256 devices in a mesh: grp: 4 (over x), tp: 32 (over y_lo, z, core), cores: 2 (over y_hi).
Axes of the slice: x: 4, y: 4 (y_hi: 2, y_lo: 2; y = y_hi * 2 + y_lo), z: 8, core: 2. Of those that a mesh axis runs over, the one named last changes fastest.
Arguments:
- tokens: bfloat16 [4096, 8192], P('grp', ('tp', 'cores')), may hold values from -6 to 6
- gate_up_weight: bfloat16 [8192, 2, 16384], P(None, None, ('tp', 'cores')), may hold values from -0.0625 to 0.0625
- down_factor_pool: bfloat16 [64, 8192, 256], P(('tp', 'cores'), 'grp'), may hold values from -0.0625 to 0.0625
- up_factor_pool: bfloat16 [64, 4, 64, 128, 128], P(('tp', 'cores'), 'grp'), may hold values from -0.5 to 0.5
- segment_adapters: int32 [4, 3], replicated, may hold values from 0 to 63
- segment_tile_counts: int32 [4, 3], P('grp'), may hold values from 1 to 4, 8 in all within a row
- adapter_pool_rows: int32 [64], replicated, may hold values from 0 to 63, each once
Outputs:
- hidden: bfloat16 [4096, 16384], P('grp', ('tp', 'cores'))
The draws below stay inside these ranges and needn't reach their ends.
Inputs may be any that keep to these rules, and one draw needn't show every extreme that they name: `segment_tile_counts`: each row sums to 8. `adapter_pool_rows`: each pool row appears once.
All inputs are finite; a program needn't handle non-finite values.
Results may differ from the reference program's by a relative error of at most 0.0036.
Values may be sent and summed in bfloat16 or wider, within the bound.
No kernel may reach another device: no remote copies, remote signals or barrier semaphores. Data moves between devices by JAX's collectives and lax.ppermute only.
A program may use at most 192 MiB of HBM per device.

```python
import math
import jax
import jax.numpy as jnp
import numpy as np
from jax import lax

MODEL_WIDTH = 8192
FF_W = 16384
ADAPTER_RANK = 128
TOKS = 1024
TILE = 128
SEGS = 3
TOKEN_GROUPS = 4
GROUP_DEVICES = 64
ADAPTER_POOL = 64
HIDDEN_SHARE_3 = 64
N_GRP = 4


def place_ends(values, key, least, largest):
    longest = values.shape.index(max(values.shape))
    spots = []
    for shift in (0, 1):
        where = [jax.random.randint(jax.random.fold_in(key, axis), (), 0, length) for axis, length in enumerate(values.shape)]
        where[longest] = (where[longest] + shift) % values.shape[longest]
        spots.append(tuple(where))
    return values.at[spots[0]].set(least).at[spots[1]].set(largest)


def levels(key, dims, cuts, low, top_value):
    def one(axis_at, shards_of):
        steps = jax.random.uniform(jax.random.fold_in(jax.random.fold_in(key, 6), axis_at), (shards_of,), jnp.float32, low / len(cuts), top_value / len(cuts))
        return jnp.repeat(jnp.exp(steps), dims[axis_at] // shards_of).reshape((-1,) + (1,) * (len(dims) - axis_at - 1))

    level = one(*cuts[0])
    for cut in cuts[1:]:
        level = level * one(*cut)
    return level


def split_up(number_of, total, most, slope):
    weights = [(1 << 20) // math.isqrt(rank ** slope) + 1 for rank in range(2, number_of + 1)]
    surplus, counts = total - most - (number_of - 1), [1] * (number_of - 1)
    while surplus > 0:
        candidates = [i for i in range(number_of - 1) if counts[i] < most]
        pool, budget = sum([weights[i] for i in candidates]), surplus
        for i in candidates:
            extra = min(most - counts[i], max(1, budget * weights[i] // pool), surplus)
            counts[i] = counts[i] + extra
            surplus = surplus - extra
    return np.array([most] + counts)


def uneven(rng, number_of, total, bound, slope):
    if number_of == 2:
        one = jax.random.randint(rng, (), max(1, total - bound), min(bound, total - 1) + 1)
        return jnp.stack([one, total - one])
    lengths = jnp.asarray(split_up(number_of, total, bound, slope), jnp.int32)
    couples = (number_of - 1) // 2
    giver, receiver = lengths[1:1 + 2 * couples:2], lengths[2:2 + 2 * couples:2]
    slack = jnp.minimum(giver - 1, bound - receiver)
    passed = jax.random.randint(jax.random.fold_in(rng, 1), (couples,), 0, 1 << 20) % (slack + 1)
    lengths = lengths.at[1:1 + 2 * couples:2].set(giver - passed).at[2:2 + 2 * couples:2].set(receiver + passed)
    return lengths[jax.random.permutation(jax.random.fold_in(rng, 2), number_of)]


def bell_draw(own_key, dims, scale, reach, cuts=(), kind=jnp.bfloat16):
    values = jax.random.normal(own_key, dims, jnp.float32) * scale
    if len(cuts) > 0:
        values = levels(own_key, dims, cuts, -0.22, 0.18) * values
    return jnp.clip(values, min=-reach, max=reach).astype(kind)


def setup_inputs(seed: int = 0) -> dict:
    seeds = jax.random.split(jax.random.key(seed), 8)
    return {
        "tokens": bell_draw(seeds[0], (TOKEN_GROUPS * TOKS, MODEL_WIDTH), 1.0, 6.0, ((0, 4), (1, 64))),
        "gate_up_weight": bell_draw(seeds[1], (MODEL_WIDTH, 2, FF_W), MODEL_WIDTH ** -0.5, 0.0625, ((2, 64),)),
        "down_factor_pool": bell_draw(seeds[2], (ADAPTER_POOL, MODEL_WIDTH, 2 * ADAPTER_RANK), MODEL_WIDTH ** -0.5, 0.0625, ((0, 64), (1, 4))),
        "up_factor_pool": bell_draw(seeds[3], (ADAPTER_POOL, TOKEN_GROUPS, GROUP_DEVICES, ADAPTER_RANK, 2 * HIDDEN_SHARE_3), ADAPTER_RANK ** -0.5, 0.5, ((0, 64), (1, 4))),
        "segment_adapters": place_ends(jax.random.randint(seeds[4], (TOKEN_GROUPS, SEGS), 0, ADAPTER_POOL), jax.random.fold_in(seeds[4], 1), 0, ADAPTER_POOL - 1).astype(jnp.int32),
        "segment_tile_counts": jax.vmap(lambda own: uneven(own, SEGS, TOKS // TILE, TOKS // TILE // 2, 1))(jax.random.split(seeds[5], TOKEN_GROUPS)).reshape((TOKEN_GROUPS, SEGS)).astype(jnp.int32),
        "adapter_pool_rows": jax.random.permutation(seeds[6], ADAPTER_POOL).astype(jnp.int32),
    }


adapter_scale = 0.5


def reference(tokens, gate_up_weight, down_factor_pool, up_factor_pool, segment_adapters, segment_tile_counts, adapter_pool_rows):
    tile_count = TOKS // TILE
    bounds = jnp.cumsum(segment_tile_counts, axis=1)
    positions = jnp.arange(tile_count, dtype=jnp.int32)
    tile_seg = jnp.sum((bounds[:, None, :] <= positions[None, :, None]).astype(jnp.int32), axis=2).astype(jnp.int32)
    tile_ids = jnp.take_along_axis(segment_adapters, tile_seg, axis=1)
    tile_rows = jnp.take(adapter_pool_rows, tile_ids.reshape(-1)).astype(jnp.int32)
    frozen_output = jnp.dot(tokens, gate_up_weight.reshape(MODEL_WIDTH, 2 * FF_W), preferred_element_type=jnp.float32)
    frozen_output = frozen_output.reshape(N_GRP * TOKS, 2, FF_W)
    token_tiles = tokens.reshape(N_GRP * tile_count, TILE, MODEL_WIDTH)

    def one_tile(item):
        token_rows_block, adapter_pool_row = item
        reduced_input = jnp.dot(token_rows_block, down_factor_pool[adapter_pool_row], preferred_element_type=jnp.float32).astype(jnp.bfloat16)
        expanded_output = up_factor_pool[adapter_pool_row].reshape(N_GRP, GROUP_DEVICES, ADAPTER_RANK, 2, HIDDEN_SHARE_3)
        expanded_output = jnp.transpose(expanded_output, (2, 3, 1, 0, 4)).reshape(ADAPTER_RANK, 2, FF_W)
        gate_part = jnp.dot(reduced_input[:, :ADAPTER_RANK], expanded_output[:, 0, :], preferred_element_type=jnp.float32)
        up_part = jnp.dot(reduced_input[:, ADAPTER_RANK:], expanded_output[:, 1, :], preferred_element_type=jnp.float32)
        return jnp.stack([gate_part, up_part], axis=1)

    adapted_output = lax.map(one_tile, (token_tiles, tile_rows)).reshape(N_GRP * TOKS, 2, FF_W)
    gate_combined = frozen_output[:, 0, :] + adapter_scale * adapted_output[:, 0, :]
    up_combined = frozen_output[:, 1, :] + adapter_scale * adapted_output[:, 1, :]
    return (jax.nn.silu(gate_combined) * up_combined).astype(jnp.bfloat16)
```

```python
import jax
import jax.numpy as jnp
from jax import lax
from jax.sharding import Mesh, PartitionSpec as P

TILE = 128
GRP = 4
YL, ZN, CORES, YH = 2, 8, 2, 2
AXES = ("grp", "ylo", "z", "core", "yhi")
PLANE = ("ylo", "z", "core", "yhi")
SHARES = YL * ZN * CORES * YH
f32 = jnp.float32
bf16 = jnp.bfloat16

adapter_scale = 0.5


def exchange(x, axes):
    return lax.all_to_all(x, axes, split_axis=0, concat_axis=0, tiled=True)


def per_device(
    tokens,
    gate_up_weight,
    down_factor_pool,
    up_factor_pool,
    segment_adapters,
    segment_tile_counts,
    adapter_pool_rows,
):
    group = lax.axis_index("grp")
    place = lax.axis_index(PLANE)
    token_count, share = tokens.shape
    tile_count = token_count // TILE
    width = gate_up_weight.shape[0]
    local_hidden = gate_up_weight.shape[2]
    twice_rank = down_factor_pool.shape[2]
    rank = twice_rank // 2
    segs = segment_adapters.shape[1]
    sub = share // GRP

    gathered = lax.all_gather(tokens, ("yhi", "ylo", "z", "core"), axis=1, tiled=True)
    w = gate_up_weight.reshape(YL * ZN * CORES, YH, share, 2 * local_hidden)
    w = jnp.transpose(w, (1, 0, 2, 3)).reshape(width, 2 * local_hidden)

    turned = tokens.T.reshape(GRP, sub, token_count)
    quarter, block = place // (SHARES // GRP), place % GRP
    own_features = []
    for k in range(GRP):
        pairs = []
        for p in range(SHARES):
            big, r = p // (SHARES // GRP), p % (SHARES // GRP)
            pairs.append((p, GRP * r + (big + k) % GRP))
        piece = lax.dynamic_index_in_dim(turned, (quarter + k) % GRP, 0, keepdims=False)
        own_features.append(lax.ppermute(piece, PLANE, pairs))
    own_features = jnp.stack(own_features).reshape(share, tile_count, TILE)

    halves = twice_rank // rank
    down_pieces = down_factor_pool.reshape(SHARES, sub, halves, rank)
    down_pieces = jnp.transpose(down_pieces, (0, 2, 1, 3)).reshape(SHARES, halves * sub, rank)
    up_pieces = up_factor_pool.reshape(SHARES, rank, rank)
    pieces = exchange(jnp.concatenate([up_pieces, down_pieces], axis=1), PLANE)
    chosen_rows = jnp.take(adapter_pool_rows, segment_adapters.reshape(-1))
    chosen = exchange(jnp.take(pieces, chosen_rows, axis=0), "grp")
    chosen = chosen.reshape(GRP, segs, rank + halves * sub, rank)
    up_chosen = chosen[:, :, :rank]
    down_chosen = chosen[:, :, rank:].reshape(GRP, segs, halves, sub, rank)
    down_chosen = jnp.take(down_chosen, (block - jnp.arange(GRP)) % GRP, axis=0)
    down_chosen = jnp.transpose(down_chosen, (1, 0, 3, 2, 4)).reshape(segs, share, twice_rank)

    bounds = jnp.cumsum(segment_tile_counts[0])
    positions = jnp.arange(tile_count, dtype=jnp.int32)
    tile_seg = jnp.sum((bounds[None, :] <= positions[:, None]).astype(jnp.int32), axis=1)

    partial = jnp.einsum(
        "dnr,ndc->nrc", own_features, jnp.take(down_chosen, tile_seg, axis=0),
        preferred_element_type=f32,
    ).astype(bf16)
    rows = token_count // SHARES
    partial = exchange(partial.reshape(SHARES, rows, twice_rank), PLANE)
    total = jnp.sum(partial.astype(f32), axis=0).astype(bf16)
    shrunk = exchange(jnp.broadcast_to(total[None], (SHARES, rows, twice_rank)), PLANE)
    shrunk = shrunk.reshape(tile_count, TILE, twice_rank)

    frozen = jnp.dot(gathered, w, preferred_element_type=f32)

    blocks = jnp.transpose(up_chosen, (1, 2, 0, 3)).reshape(segs, rank, GRP, 2, rank // 2)
    gate_blocks = jnp.take(blocks[:, :, :, 0].reshape(segs, rank, local_hidden), tile_seg, axis=0)
    up_blocks = jnp.take(blocks[:, :, :, 1].reshape(segs, rank, local_hidden), tile_seg, axis=0)
    gate_delta = jnp.einsum(
        "tkr,trw->tkw", shrunk[:, :, :rank], gate_blocks, preferred_element_type=f32
    ).reshape(token_count, local_hidden)
    up_delta = jnp.einsum(
        "tkr,trw->tkw", shrunk[:, :, rank:], up_blocks, preferred_element_type=f32
    ).reshape(token_count, local_hidden)
    gate = frozen[:, :local_hidden] + adapter_scale * gate_delta
    up = frozen[:, local_hidden:] + adapter_scale * up_delta
    return (jax.nn.silu(gate) * up).astype(bf16)


def solution(mesh):
    fine = Mesh(mesh.devices.reshape(GRP, YL, ZN, CORES, YH), AXES)
    return jax.shard_map(
        per_device,
        mesh=fine,
        in_specs=(
            P("grp", PLANE),
            P(None, None, PLANE),
            P(PLANE, "grp", None),
            P(PLANE, "grp", None, None, None),
            P(),
            P("grp", None),
            P(),
        ),
        out_specs=P("grp", PLANE),
        check_vma=False,
    )
```

```python
import jax
import jax.numpy as jnp
from jax import lax
from jax.sharding import Mesh, PartitionSpec as P

TILE = 128
GRP = 4
YL, ZN, CORES, YH = 2, 8, 2, 2
AXES = ("grp", "ylo", "z", "core", "yhi")
PLANE = ("ylo", "z", "core", "yhi")
SHARES = YL * ZN * CORES * YH
f32 = jnp.float32
bf16 = jnp.bfloat16

adapter_scale = 0.5


def exchange(x, axes):
    return lax.all_to_all(x, axes, split_axis=0, concat_axis=0, tiled=True)


def per_device(
    tokens,
    gate_up_weight,
    down_factor_pool,
    up_factor_pool,
    segment_adapters,
    segment_tile_counts,
    adapter_pool_rows,
):
    token_count, share = tokens.shape
    tile_count = token_count // TILE
    width = gate_up_weight.shape[0]
    local_hidden = gate_up_weight.shape[2]
    twice_rank = down_factor_pool.shape[2]
    rank = twice_rank // 2
    segs = segment_adapters.shape[1]

    gathered = lax.all_gather(tokens, ("yhi", "ylo", "z", "core"), axis=1, tiled=True)
    w = gate_up_weight.reshape(YL * ZN * CORES, YH, share, 2 * local_hidden)
    w = jnp.transpose(w, (1, 0, 2, 3)).reshape(width, 2 * local_hidden)

    chosen_rows = jnp.take(adapter_pool_rows, segment_adapters.reshape(-1), mode="clip")
    up_pieces = exchange(up_factor_pool.reshape(SHARES, rank, rank), PLANE)
    up_chosen = exchange(jnp.take(up_pieces, chosen_rows, axis=0, mode="clip"), "grp")
    up_chosen = up_chosen.reshape(GRP, segs, rank, rank)

    cols = twice_rank // SHARES
    quarter_rows = down_factor_pool.shape[1]
    down_pieces = exchange(down_factor_pool[0].T.reshape(SHARES, cols, quarter_rows), PLANE)
    down_chosen = exchange(jnp.take(down_pieces, chosen_rows, axis=0, mode="clip"), "grp")
    down_chosen = down_chosen.reshape(YL, GRP // YL, segs, cols, -1, CORES, YH, share)
    down_chosen = jnp.transpose(down_chosen, (2, 3, 6, 0, 1, 4, 5, 7)).reshape(segs * cols, width)

    bounds = jnp.cumsum(segment_tile_counts[0])
    positions = jnp.arange(tile_count, dtype=jnp.int32)
    tile_seg = jnp.sum((bounds[None, :] <= positions[:, None]).astype(jnp.int32), axis=1)

    blocks = jnp.transpose(up_chosen, (1, 2, 0, 3)).reshape(segs, rank, GRP, 2, rank // 2)
    gate_blocks = jnp.take(blocks[:, :, :, 0].reshape(segs, rank, local_hidden), tile_seg, axis=0, mode="clip")
    up_blocks = jnp.take(blocks[:, :, :, 1].reshape(segs, rank, local_hidden), tile_seg, axis=0, mode="clip")

    down_chosen, w, gate_blocks, up_blocks = lax.optimization_barrier(
        (down_chosen, w, gate_blocks, up_blocks)
    )

    columns = lax.dot_general(
        down_chosen, gathered, (((1,), (1,)), ((), ())), preferred_element_type=f32
    ).reshape(segs, cols, tile_count, TILE)
    own_seg = tile_seg[None, :] == jnp.arange(segs, dtype=jnp.int32)[:, None]
    columns = jnp.sum(jnp.where(own_seg[:, None, :, None], columns, 0.0), axis=0).astype(bf16)
    columns = columns.reshape(cols, token_count)
    shrunk = exchange(jnp.broadcast_to(columns[None], (SHARES, cols, token_count)), PLANE)
    shrunk = shrunk.reshape(twice_rank, tile_count, TILE)

    frozen = jnp.dot(gathered, w, preferred_element_type=f32)

    gate_delta = jnp.einsum(
        "rtk,trw->tkw", shrunk[:rank], gate_blocks, preferred_element_type=f32
    ).reshape(token_count, local_hidden)
    up_delta = jnp.einsum(
        "rtk,trw->tkw", shrunk[rank:], up_blocks, preferred_element_type=f32
    ).reshape(token_count, local_hidden)
    gate = frozen[:, :local_hidden] + adapter_scale * gate_delta
    up = frozen[:, local_hidden:] + adapter_scale * up_delta
    return (jax.nn.silu(gate) * up).astype(bf16)


def solution(mesh):
    fine = Mesh(mesh.devices.reshape(GRP, YL, ZN, CORES, YH), AXES)
    return jax.shard_map(
        per_device,
        mesh=fine,
        in_specs=(
            P("grp", PLANE),
            P(None, None, PLANE),
            P(PLANE, "grp", None),
            P(PLANE, "grp", None, None, None),
            P(),
            P("grp", None),
            P(),
        ),
        out_specs=P("grp", PLANE),
        check_vma=False,
    )
```

```python
import jax
import jax.numpy as jnp
from jax import lax
from jax.experimental import pallas as pl
from jax.experimental.pallas import tpu as pltpu
from jax.sharding import Mesh, PartitionSpec as P

TILE = 128
GRP = 4
YL, ZN, CORES, YH = 2, 8, 2, 2
AXES = ("grp", "ylo", "z", "core", "yhi")
PLANE = ("ylo", "z", "core", "yhi")
SHARES = YL * ZN * CORES * YH
f32 = jnp.float32
bf16 = jnp.bfloat16

adapter_scale = 0.5

SLOT = 8
STEPS = 8


def shrink_kernel(tile_seg, tokens, columns, out, total):
    step = pl.program_id(0)

    @pl.when(step == 0)
    def _():
        total[...] = jnp.zeros_like(total)

    total[...] += lax.dot_general(
        tokens[...], columns[...], (((1,), (1,)), ((), ())), preferred_element_type=f32
    )

    @pl.when(step == pl.num_programs(0) - 1)
    def _():
        turned = total[...].T
        for i in range(out.shape[1] // TILE):
            seg = tile_seg[i]
            at = slice(i * TILE, (i + 1) * TILE)
            pick = turned[:SLOT, at]
            for j in range(1, columns.shape[0] // SLOT):
                pick = jnp.where(seg == j, turned[j * SLOT : (j + 1) * SLOT, at], pick)
            out[:, at] = pick


def shrink(tokens, columns, tile_seg):
    count, width = tokens.shape
    slots = columns.shape[0]
    part = width // STEPS
    return pl.pallas_call(
        shrink_kernel,
        out_shape=jax.ShapeDtypeStruct((SLOT, count), f32),
        grid_spec=pltpu.PrefetchScalarGridSpec(
            num_scalar_prefetch=1,
            grid=(STEPS,),
            in_specs=[
                pl.BlockSpec((count, part), lambda k, seg: (0, k)),
                pl.BlockSpec((slots, part), lambda k, seg: (0, k)),
            ],
            out_specs=pl.BlockSpec((SLOT, count), lambda k, seg: (0, 0)),
            scratch_shapes=[pltpu.VMEM((count, slots), f32)],
        ),
        compiler_params=pltpu.CompilerParams(
            dimension_semantics=("arbitrary",), vmem_limit_bytes=60 << 20
        ),
        name="shrink",
    )(tile_seg, tokens, columns)


def frozen_kernel(tokens, weight, out):
    part = jnp.dot(tokens[...], weight[...], preferred_element_type=f32)

    @pl.when(pl.program_id(0) == 0)
    def _():
        out[...] = part

    @pl.when(pl.program_id(0) > 0)
    def _():
        out[...] += part


def frozen_matmul(tokens, weight):
    count, width = tokens.shape
    wide = weight.shape[1]
    part = width // STEPS
    return pl.pallas_call(
        frozen_kernel,
        out_shape=jax.ShapeDtypeStruct((count, wide), f32),
        grid=(STEPS,),
        in_specs=[
            pl.BlockSpec((count, part), lambda k: (0, k)),
            pl.BlockSpec((part, wide), lambda k: (k, 0)),
        ],
        out_specs=pl.BlockSpec((count, wide), lambda k: (0, 0)),
        compiler_params=pltpu.CompilerParams(
            dimension_semantics=("arbitrary",), vmem_limit_bytes=60 << 20
        ),
        name="frozen",
    )(tokens, weight)


def adapt_kernel(tile_seg, frozen, shrunk, factors, out):
    rank = factors.shape[2]
    hidden = out.shape[1]
    low = lax.broadcasted_iota(jnp.int32, (TILE, rank), 1) < rank // 2
    for_gate = shrunk[:rank, :].astype(f32).T.astype(bf16)
    for_up = shrunk[rank:, :].astype(f32).T.astype(bf16)

    def expand(left, m):
        return jnp.dot(left, factors[m, 0], preferred_element_type=f32)

    for a in range(hidden // rank):
        at = slice(a * rank, (a + 1) * rank)
        gate = jnp.where(
            low, expand(for_gate, 2 * a), pltpu.roll(expand(for_gate, 2 * a + 1), rank // 2, 1)
        )
        up = jnp.where(
            low, pltpu.roll(expand(for_up, 2 * a), rank // 2, 1), expand(for_up, 2 * a + 1)
        )
        gate = frozen[:, at] + adapter_scale * gate
        up = frozen[:, hidden + a * rank : hidden + (a + 1) * rank] + adapter_scale * up
        out[:, at] = (gate / (1.0 + jnp.exp(-gate)) * up).astype(bf16)


def adapt(frozen, shrunk, factors, tile_seg):
    count, wide = frozen.shape
    parts, _, rank, _ = factors.shape
    return pl.pallas_call(
        adapt_kernel,
        out_shape=jax.ShapeDtypeStruct((count, wide // 2), bf16),
        grid_spec=pltpu.PrefetchScalarGridSpec(
            num_scalar_prefetch=1,
            grid=(count // TILE,),
            in_specs=[
                pl.BlockSpec((TILE, wide), lambda i, seg: (i, 0)),
                pl.BlockSpec((2 * rank, TILE), lambda i, seg: (0, i)),
                pl.BlockSpec((parts, 1, rank, rank), lambda i, seg: (0, seg[i], 0, 0)),
            ],
            out_specs=pl.BlockSpec((TILE, wide // 2), lambda i, seg: (i, 0)),
        ),
        compiler_params=pltpu.CompilerParams(
            dimension_semantics=("arbitrary",), vmem_limit_bytes=60 << 20
        ),
        name="adapt",
    )(tile_seg, frozen, shrunk, factors)


def exchange(x, axes):
    return lax.all_to_all(x, axes, split_axis=0, concat_axis=0, tiled=True)


def per_device(
    tokens,
    gate_up_weight,
    down_factor_pool,
    up_factor_pool,
    segment_adapters,
    segment_tile_counts,
    adapter_pool_rows,
):
    token_count, share = tokens.shape
    tile_count = token_count // TILE
    width = gate_up_weight.shape[0]
    local_hidden = gate_up_weight.shape[2]
    twice_rank = down_factor_pool.shape[2]
    rank = twice_rank // 2
    segs = segment_adapters.shape[1]

    gathered = lax.all_gather(tokens, ("yhi", "ylo", "z", "core"), axis=1, tiled=True)
    w = gate_up_weight.reshape(YL * ZN * CORES, YH, share, 2 * local_hidden)
    w = jnp.transpose(w, (1, 0, 2, 3)).reshape(width, 2 * local_hidden)

    bounds = jnp.cumsum(segment_tile_counts[0])
    positions = jnp.arange(tile_count, dtype=jnp.int32)
    tile_seg = jnp.sum((bounds[None, :] <= positions[:, None]).astype(jnp.int32), axis=1)
    chosen_rows = jnp.take(adapter_pool_rows, segment_adapters.reshape(-1), mode="clip")

    cols = twice_rank // SHARES
    quarter_rows = down_factor_pool.shape[1]
    down_pieces = exchange(down_factor_pool[0].T.reshape(SHARES, cols, quarter_rows), PLANE)
    columns = exchange(jnp.take(down_pieces, chosen_rows, axis=0, mode="clip"), "grp")
    columns = columns.reshape(YL, GRP // YL, segs, cols, -1, CORES, YH, share)
    columns = jnp.transpose(columns, (2, 3, 6, 0, 1, 4, 5, 7)).reshape(segs, cols, width)
    columns = jnp.pad(columns, ((0, 1), (0, SLOT - cols), (0, 0))).reshape(-1, width)

    up_pieces = exchange(up_factor_pool.reshape(SHARES, rank, rank), PLANE)
    up_chosen = exchange(jnp.take(up_pieces, chosen_rows, axis=0, mode="clip"), "grp")
    up_chosen = up_chosen.reshape(GRP, segs, rank, rank)
    columns, w, up_chosen = lax.optimization_barrier((columns, w, up_chosen))

    own_columns = shrink(gathered, columns, tile_seg)[:cols].astype(bf16)
    shrunk = exchange(jnp.broadcast_to(own_columns[None], (SHARES, cols, token_count)), PLANE)

    frozen = frozen_matmul(gathered, w)
    return adapt(frozen, shrunk.reshape(twice_rank, token_count), up_chosen, tile_seg)


def solution(mesh):
    fine = Mesh(mesh.devices.reshape(GRP, YL, ZN, CORES, YH), AXES)
    return jax.shard_map(
        per_device,
        mesh=fine,
        in_specs=(
            P("grp", PLANE),
            P(None, None, PLANE),
            P(PLANE, "grp", None),
            P(PLANE, "grp", None, None, None),
            P(),
            P("grp", None),
            P(),
        ),
        out_specs=P("grp", PLANE),
        check_vma=False,
    )
```

```python
import jax
import jax.numpy as jnp
from jax import lax
from jax.experimental import pallas as pl
from jax.experimental.pallas import tpu as pltpu
from jax.sharding import Mesh, PartitionSpec as P

TILE = 128
GRP = 4
YL, ZN, CORES, YH = 2, 8, 2, 2
AXES = ("grp", "ylo", "z", "core", "yhi")
PLANE = ("ylo", "z", "core", "yhi")
LINE = ("ylo", "core", "yhi")
SHARES = YL * ZN * CORES * YH
f32 = jnp.float32
bf16 = jnp.bfloat16

adapter_scale = 0.5

SLOT = 8
ROUND = 4
STEPS = 4


def shrink_kernel(tile_seg, tokens, columns, out, total):
    step = pl.program_id(0)
    part = lax.dot_general(
        columns[...], tokens[...], (((1,), (1,)), ((), ())), preferred_element_type=f32
    )

    @pl.when(step == 0)
    def _():
        total[...] = part

    @pl.when(step > 0)
    def _():
        total[...] += part

    @pl.when(step == pl.num_programs(0) - 1)
    def _():
        for i in range(out.shape[1] // TILE):
            seg = tile_seg[i]
            at = slice(i * TILE, (i + 1) * TILE)
            pick = total[:SLOT, at]
            for j in range(1, columns.shape[0] // SLOT):
                pick = jnp.where(seg == j, total[j * SLOT : (j + 1) * SLOT, at], pick)
            out[:, at] = pick


def shrink(tokens, columns, tile_seg):
    count, width = tokens.shape
    slots = columns.shape[0]
    part = width // STEPS
    return pl.pallas_call(
        shrink_kernel,
        out_shape=jax.ShapeDtypeStruct((SLOT, count), f32),
        grid_spec=pltpu.PrefetchScalarGridSpec(
            num_scalar_prefetch=1,
            grid=(STEPS,),
            in_specs=[
                pl.BlockSpec((count, part), lambda k, seg: (0, k)),
                pl.BlockSpec((slots, part), lambda k, seg: (0, k)),
            ],
            out_specs=pl.BlockSpec((SLOT, count), lambda k, seg: (0, 0)),
            scratch_shapes=[pltpu.VMEM((slots, count), f32)],
        ),
        compiler_params=pltpu.CompilerParams(
            dimension_semantics=("arbitrary",), vmem_limit_bytes=60 << 20
        ),
        name="shrink",
    )(tile_seg, tokens, columns)


def frozen_kernel(tokens, weight, out):
    part = jnp.dot(tokens[...], weight[...], preferred_element_type=f32)

    @pl.when(pl.program_id(0) == 0)
    def _():
        out[...] = part

    @pl.when(pl.program_id(0) > 0)
    def _():
        out[...] += part


def frozen_matmul(tokens, weight):
    count, width = tokens.shape
    wide = weight.shape[1]
    part = width // STEPS
    return pl.pallas_call(
        frozen_kernel,
        out_shape=jax.ShapeDtypeStruct((count, wide), f32),
        grid=(STEPS,),
        in_specs=[
            pl.BlockSpec((count, part), lambda k: (0, k)),
            pl.BlockSpec((part, wide), lambda k: (k, 0)),
        ],
        out_specs=pl.BlockSpec((count, wide), lambda k: (0, 0)),
        compiler_params=pltpu.CompilerParams(
            dimension_semantics=("arbitrary",), vmem_limit_bytes=60 << 20
        ),
        name="frozen",
    )(tokens, weight)


def adapt_kernel(tile_seg, frozen, shrunk, factors, out):
    parts, _, rank, _ = factors.shape
    hidden = out.shape[1]
    tiles = out.shape[0] // TILE
    low = lax.broadcasted_iota(jnp.int32, (TILE, rank), 1) < rank // 2
    for t in range(tiles):
        seg = tile_seg[pl.program_id(0) * tiles + t]
        rows = slice(t * TILE, (t + 1) * TILE)
        wide = jnp.concatenate([factors[m, seg] for m in range(parts)], axis=1)
        left = shrunk[:, rows].astype(f32)
        for_gate = jnp.dot(left[:rank].T.astype(bf16), wide, preferred_element_type=f32)
        for_up = jnp.dot(left[rank:].T.astype(bf16), wide, preferred_element_type=f32)
        for a in range(parts // 2):
            even = slice(2 * a * rank, (2 * a + 1) * rank)
            odd = slice((2 * a + 1) * rank, (2 * a + 2) * rank)
            at = slice(a * rank, (a + 1) * rank)
            gate = jnp.where(low, for_gate[:, even], pltpu.roll(for_gate[:, odd], rank // 2, 1))
            up = jnp.where(low, pltpu.roll(for_up[:, even], rank // 2, 1), for_up[:, odd])
            gate = frozen[rows, at] + adapter_scale * gate
            up = frozen[rows, hidden + a * rank : hidden + (a + 1) * rank] + adapter_scale * up
            out[rows, at] = (gate / (1.0 + jnp.exp(-gate)) * up).astype(bf16)


def adapt(frozen, shrunk, factors, tile_seg):
    count, wide = frozen.shape
    rows = count // STEPS
    return pl.pallas_call(
        adapt_kernel,
        out_shape=jax.ShapeDtypeStruct((count, wide // 2), bf16),
        grid_spec=pltpu.PrefetchScalarGridSpec(
            num_scalar_prefetch=1,
            grid=(STEPS,),
            in_specs=[
                pl.BlockSpec((rows, wide), lambda i, seg: (i, 0)),
                pl.BlockSpec((shrunk.shape[0], rows), lambda i, seg: (0, i)),
                pl.BlockSpec(factors.shape, lambda i, seg: (0, 0, 0, 0)),
            ],
            out_specs=pl.BlockSpec((rows, wide // 2), lambda i, seg: (i, 0)),
        ),
        compiler_params=pltpu.CompilerParams(
            dimension_semantics=("arbitrary",), vmem_limit_bytes=60 << 20
        ),
        name="adapt",
    )(tile_seg, frozen, shrunk, factors)


def exchange(x, axes):
    return lax.all_to_all(x, axes, split_axis=0, concat_axis=0, tiled=True)


def per_device(
    tokens,
    gate_up_weight,
    down_factor_pool,
    up_factor_pool,
    segment_adapters,
    segment_tile_counts,
    adapter_pool_rows,
):
    token_count, share = tokens.shape
    tile_count = token_count // TILE
    width = gate_up_weight.shape[0]
    local_hidden = gate_up_weight.shape[2]
    twice_rank = down_factor_pool.shape[2]
    rank = twice_rank // 2
    segs = segment_adapters.shape[1]

    gathered = lax.all_gather(tokens, ("yhi", "ylo", "z", "core"), axis=1, tiled=True)
    w = gate_up_weight.reshape(YL * ZN * CORES, YH, share, 2 * local_hidden)
    w = jnp.transpose(w, (1, 0, 2, 3)).reshape(width, 2 * local_hidden)

    bounds = jnp.cumsum(segment_tile_counts[0])
    positions = jnp.arange(tile_count, dtype=jnp.int32)
    tile_seg = jnp.sum((bounds[None, :] <= positions[:, None]).astype(jnp.int32), axis=1)
    chosen_rows = jnp.take(adapter_pool_rows, segment_adapters.reshape(-1), mode="clip")

    cols = twice_rank // SHARES
    depth = rank + share // 2
    line = SHARES // ZN
    down_pool = down_factor_pool[0].T.reshape(SHARES, cols, -1, share)
    down_pool = jnp.transpose(down_pool, (0, 2, 1, 3)).reshape(SHARES, depth - rank, share)
    pool = jnp.concatenate([up_factor_pool.reshape(SHARES, rank, rank), down_pool], axis=1)

    pool = pool.reshape(YL, ZN, CORES, YH, depth, share)
    pool = jnp.transpose(pool, (0, 2, 3, 1, 4, 5)).reshape(line, ZN, depth, share)
    pool = exchange(pool, LINE)
    pool, w = lax.optimization_barrier((pool, w))

    row_z = (chosen_rows // (CORES * YH)) % ZN
    row_at = chosen_rows // (ZN * CORES * YH) * (CORES * YH) + chosen_rows % (CORES * YH)
    used = (row_z[:, None, None] == jnp.arange(ZN)[None, :, None]) & (
        row_at[:, None, None] == jnp.arange(line)[None, None, :]
    )
    used = jnp.any(used, axis=0).astype(jnp.int32)
    earlier = jnp.arange(line)[:, None] < jnp.arange(line)[None, :]
    order = jnp.sum(used[:, :, None] * earlier.astype(jnp.int32)[None], axis=1)
    rounds = (jnp.max(jnp.sum(used, axis=1)) + ROUND - 1) // ROUND
    here = (row_z[:, None, None] == jnp.arange(ZN)[None, :, None]) & (
        row_at[:, None, None] == jnp.arange(line)[None, None, :]
    )
    slot_order = jnp.sum(jnp.where(here, order[None], 0), axis=(1, 2))
    own_line = jnp.arange(ZN)[:, None] == lax.axis_index("z")
    own_used = jnp.sum(jnp.where(own_line, used, 0), axis=0)
    own_order = jnp.sum(jnp.where(own_line, order, 0), axis=0)

    def fetch(turn):
        wanted = turn * ROUND + jnp.arange(ROUND)
        hit = (own_used[None, :] > 0) & (own_order[None, :] == wanted[:, None])
        rows = jnp.sum(jnp.where(hit, jnp.arange(line)[None, :], 0), axis=1)
        sent = jnp.take(pool, rows, axis=0, mode="clip")
        sent = exchange(jnp.transpose(sent, (1, 0, 2, 3)), "z").reshape(-1, depth, share)
        at = row_z * ROUND + jnp.clip(slot_order - turn * ROUND, 0, ROUND - 1)
        return jnp.take(sent, at, axis=0, mode="clip")

    def again(carry):
        turn, chosen = carry
        fresh = (slot_order >= turn * ROUND)[:, None, None]
        return turn + 1, jnp.where(fresh, fetch(turn), chosen)

    chosen = lax.while_loop(lambda carry: carry[0] < rounds, again, (1, fetch(0)))[1]

    chosen = exchange(chosen, "grp").reshape(GRP, segs, depth, share)
    up_chosen = chosen[:, :, :rank]
    columns = chosen[:, :, rank:].reshape(YL, GRP // YL, segs, -1, CORES, YH, cols, share)
    columns = jnp.transpose(columns, (2, 6, 5, 0, 1, 3, 4, 7)).reshape(segs, cols, width)
    columns = jnp.pad(columns, ((0, 1), (0, SLOT - cols), (0, 0))).reshape(-1, width)
    columns, up_chosen = lax.optimization_barrier((columns, up_chosen))

    own_columns = shrink(gathered, columns, tile_seg)[:cols].astype(bf16)
    shrunk = exchange(jnp.broadcast_to(own_columns[None], (SHARES, cols, token_count)), PLANE)

    frozen = frozen_matmul(gathered, w)
    return adapt(frozen, shrunk.reshape(twice_rank, token_count), up_chosen, tile_seg)


def solution(mesh):
    fine = Mesh(mesh.devices.reshape(GRP, YL, ZN, CORES, YH), AXES)
    return jax.shard_map(
        per_device,
        mesh=fine,
        in_specs=(
            P("grp", PLANE),
            P(None, None, PLANE),
            P(PLANE, "grp", None),
            P(PLANE, "grp", None, None, None),
            P(),
            P("grp", None),
            P(),
        ),
        out_specs=P("grp", PLANE),
        check_vma=False,
    )
```

```python
import functools

import jax
import jax.numpy as jnp
from jax import lax
from jax.experimental import pallas as pl
from jax.experimental.pallas import tpu as pltpu
from jax.sharding import Mesh, PartitionSpec as P

TILE = 128
GRP = 4
YL, ZN, CORES, YH = 2, 8, 2, 2
AXES = ("grp", "ylo", "z", "core", "yhi")
PLANE = ("ylo", "z", "core", "yhi")
CHIPS = ("ylo", "z", "yhi")
SHARES = YL * ZN * CORES * YH
f32 = jnp.float32
bf16 = jnp.bfloat16

adapter_scale = 0.5

SLOT = 8
DEEP = 4


def pieces_of(refs, counts, halved):
    parts, at = [], 0
    for n, half in zip(counts, halved):
        if half:
            top, bottom = refs[at], refs[at + 1]
            at += 2
            rows = top.shape[1]
            parts += [[(top, i, 0, rows), (bottom, i, rows, rows)] for i in range(n)]
        else:
            rows = refs[at].shape[1]
            parts += [[(refs[at], i, 0, rows)] for i in range(n)]
            at += 1
    return parts


def shrink_kernel(counts, halved, chip, tile_seg, columns, *refs):
    chunks, out, buffer, sems = refs[:-3], refs[-3], refs[-2], refs[-1]
    parts = pieces_of(chunks, counts, halved)

    def copies(k):
        slot = k % DEEP
        return [
            pltpu.make_async_copy(
                ref.at[i], buffer.at[slot, pl.ds(first, rows)], sems.at[slot, j]
            )
            for j, (ref, i, first, rows) in enumerate(parts[k])
        ]

    for k in range(DEEP):
        for copy in copies(k):
            copy.start()
    total = jnp.zeros((columns.shape[1], buffer.shape[1]), f32)
    for k in range(len(parts)):
        for copy in copies(k):
            copy.wait()
        total += lax.dot_general(
            columns[chip[k]],
            buffer[k % DEEP],
            (((1,), (1,)), ((), ())),
            preferred_element_type=f32,
        )
        if k + DEEP < len(parts):
            for copy in copies(k + DEEP):
                copy.start()
    per = columns.shape[1] // CORES
    for c in range(CORES):
        for i in range(out.shape[2] // TILE):
            seg = tile_seg[i]
            at = slice(i * TILE, (i + 1) * TILE)
            pick = total[c * per : c * per + SLOT, at]
            for j in range(1, per // SLOT):
                low = c * per + j * SLOT
                pick = jnp.where(seg == j, total[low : low + SLOT, at], pick)
            out[c, :, at] = pick


def shrink(chunks, counts, halved, columns, chip, tile_seg, rows, width):
    most = 2
    return pl.pallas_call(
        functools.partial(shrink_kernel, counts, halved),
        out_shape=jax.ShapeDtypeStruct((CORES, SLOT, rows), f32),
        grid_spec=pltpu.PrefetchScalarGridSpec(
            num_scalar_prefetch=2,
            grid=(1,),
            in_specs=[pl.BlockSpec(columns.shape, lambda i, a, b: (0, 0, 0))]
            + [pl.BlockSpec(memory_space=pl.ANY)] * len(chunks),
            out_specs=pl.BlockSpec((CORES, SLOT, rows), lambda i, a, b: (0, 0, 0)),
            scratch_shapes=[
                pltpu.VMEM((DEEP, rows, width), bf16),
                pltpu.SemaphoreType.DMA((DEEP, most)),
            ],
        ),
        compiler_params=pltpu.CompilerParams(vmem_limit_bytes=56 << 20),
        name="shrink",
    )(chip, tile_seg, columns, *chunks)


def frozen_kernel(counts, halved, first_block, own, other, *refs):
    chunks = refs[:-4]
    out, buffer, weights, sems = refs[-4:]
    parts = pieces_of(chunks, counts, halved)
    share = own.shape[1]

    def copies(k):
        slot = k % DEEP
        made = [
            (ref.at[i], buffer.at[slot, pl.ds(first, rows)])
            for ref, i, first, rows in parts[k]
        ]
        for c in range(CORES):
            block = first_block[k] + YH * c
            for which, source in enumerate((own, other)):
                made.append(
                    (source.at[block], weights.at[slot, which, pl.ds(c * share, share)])
                )
        return [
            pltpu.make_async_copy(a, b, sems.at[slot, j]) for j, (a, b) in enumerate(made)
        ]

    for k in range(DEEP):
        for copy in copies(k):
            copy.start()
    for k in range(len(parts)):
        for copy in copies(k):
            copy.wait()
        slot = k % DEEP
        for which in range(CORES):
            part = jnp.dot(buffer[slot], weights[slot, which], preferred_element_type=f32)
            if k == 0:
                out[which] = part
            else:
                out[which] += part
        if k + DEEP < len(parts):
            for copy in copies(k + DEEP):
                copy.start()


def frozen_matmul(chunks, counts, halved, own, other, first_block, rows, width):
    share, wide = own.shape[1:]
    shape = (CORES, rows, wide)
    return pl.pallas_call(
        functools.partial(frozen_kernel, counts, halved),
        out_shape=jax.ShapeDtypeStruct(shape, f32),
        grid_spec=pltpu.PrefetchScalarGridSpec(
            num_scalar_prefetch=1,
            grid=(1,),
            in_specs=[pl.BlockSpec(memory_space=pl.ANY)] * (2 + len(chunks)),
            out_specs=pl.BlockSpec(shape, lambda i, a: (0, 0, 0)),
            scratch_shapes=[
                pltpu.VMEM((DEEP, rows, width), bf16),
                pltpu.VMEM((DEEP, CORES, width, wide), bf16),
                pltpu.SemaphoreType.DMA((DEEP, 2 + 2 * CORES)),
            ],
        ),
        compiler_params=pltpu.CompilerParams(vmem_limit_bytes=56 << 20),
        name="frozen",
    )(first_block, own, other, *chunks)


def adapt_kernel(tile_seg, frozen, shrunk, own, other, out):
    parts, _, rank, _ = own.shape
    hidden = out.shape[2]
    low = lax.broadcasted_iota(jnp.int32, (TILE, rank), 1) < rank // 2
    seg = tile_seg[pl.program_id(0)]
    left = shrunk[...].astype(f32)
    gate_left = left[:rank].T.astype(bf16)
    up_left = left[rank:].T.astype(bf16)
    for which, factors in enumerate((own, other)):
        wide = jnp.concatenate([factors[m, seg] for m in range(parts)], axis=1)
        for_gate = jnp.dot(gate_left, wide, preferred_element_type=f32)
        for_up = jnp.dot(up_left, wide, preferred_element_type=f32)
        for a in range(parts // 2):
            even = slice(2 * a * rank, (2 * a + 1) * rank)
            odd = slice((2 * a + 1) * rank, (2 * a + 2) * rank)
            at = slice(a * rank, (a + 1) * rank)
            gate = jnp.where(low, for_gate[:, even], pltpu.roll(for_gate[:, odd], rank // 2, 1))
            up = jnp.where(low, pltpu.roll(for_up[:, even], rank // 2, 1), for_up[:, odd])
            gate = frozen[which, :, at] + adapter_scale * gate
            up = frozen[which, :, hidden + a * rank : hidden + (a + 1) * rank] + adapter_scale * up
            out[which, :, at] = (gate / (1.0 + jnp.exp(-gate)) * up).astype(bf16)


def adapt(frozen, shrunk, own, other, tile_seg):
    both, count, wide = frozen.shape
    whole = pl.BlockSpec(own.shape, lambda i, seg: (0, 0, 0, 0))
    return pl.pallas_call(
        adapt_kernel,
        out_shape=jax.ShapeDtypeStruct((both, count, wide // 2), bf16),
        grid_spec=pltpu.PrefetchScalarGridSpec(
            num_scalar_prefetch=1,
            grid=(count // TILE,),
            in_specs=[
                pl.BlockSpec((both, TILE, wide), lambda i, seg: (0, i, 0)),
                pl.BlockSpec((shrunk.shape[0], TILE), lambda i, seg: (0, i)),
                whole,
                whole,
            ],
            out_specs=pl.BlockSpec((both, TILE, wide // 2), lambda i, seg: (0, i, 0)),
        ),
        compiler_params=pltpu.CompilerParams(
            dimension_semantics=("arbitrary",), vmem_limit_bytes=56 << 20
        ),
        name="adapt",
    )(tile_seg, frozen, shrunk, own, other)


def exchange(x, axes):
    return lax.all_to_all(x, axes, split_axis=0, concat_axis=0, tiled=True)


def swap(x):
    return lax.ppermute(x, "core", [(0, 1), (1, 0)])


def shift_z(x, by):
    return lax.ppermute(x, "z", [(i, (i + by) % ZN) for i in range(ZN)])


def shift_y(x, by):
    at = [y % YL * YH + y // YL for y in range(YL * YH)]
    return lax.ppermute(x, ("ylo", "yhi"), [(at[y], at[(y + by) % len(at)]) for y in range(len(at))])


def per_device(
    tokens,
    gate_up_weight,
    down_factor_pool,
    up_factor_pool,
    segment_adapters,
    segment_tile_counts,
    adapter_pool_rows,
):
    core = lax.axis_index("core")
    my_z = lax.axis_index("z")
    my_y = lax.axis_index("yhi") * YL + lax.axis_index("ylo")
    token_count, share = tokens.shape
    tile_count = token_count // TILE
    width = gate_up_weight.shape[0]
    wide = 2 * gate_up_weight.shape[2]
    twice_rank = down_factor_pool.shape[2]
    rank = twice_rank // 2
    segs = segment_adapters.shape[1]
    rows = token_count // CORES
    both = CORES * share

    kept = lax.dynamic_slice_in_dim(tokens, core * rows, rows, axis=0)
    given = swap(lax.dynamic_slice_in_dim(tokens, (1 - core) * rows, rows, axis=0))
    first = core == 0
    start = jnp.concatenate(
        [jnp.where(first, kept, given), jnp.where(first, given, kept)], axis=1
    )[None]

    cols = twice_rank // SHARES
    depth = rank + share // 2
    down_pool, start = lax.optimization_barrier((down_factor_pool[0], start))
    down_pool = down_pool.T.reshape(SHARES, cols, -1, share)
    down_pool = jnp.transpose(down_pool, (0, 2, 1, 3)).reshape(SHARES, depth - rank, share)
    pool = jnp.concatenate([up_factor_pool.reshape(SHARES, rank, rank), down_pool], axis=1)

    half = rows // 2
    ahead, back = [start], [start]
    for k in range(ZN // 2 - 1):
        ahead.append(shift_z(ahead[-1], 1))
        back.append(shift_z(back[-1], -1))
        if k == 0:
            pool, gate_up_weight, ahead[1], back[1] = lax.optimization_barrier(
                (pool, gate_up_weight, ahead[1], back[1])
            )
            own_weight = gate_up_weight.reshape(SHARES, share, wide)
            near = jnp.concatenate([start, ahead[1], back[1]])
        if k == 1:
            near, own_weight, ahead[2], back[2] = lax.optimization_barrier(
                (near, own_weight, ahead[2], back[2])
            )
    far = jnp.concatenate(
        [shift_z(ahead[-1][:, :half], 1), shift_z(back[-1][:, half:], -1)], axis=1
    )
    sets = [
        (near, (0, -1, 1)),
        (jnp.concatenate([ahead[2], back[2], ahead[3], back[3]]), (-2, 2, -3, 3)),
        (far, (4,)),
    ]

    chunks, counts, halved, steps = [], [], [], []
    for group, away in sets:
        if len(chunks) == 5:
            group, chunks[1], chunks[2] = lax.optimization_barrier((group, chunks[1], chunks[2]))
        ahead_y, back_y = shift_y(group, 1), shift_y(group, -1)
        far_y = [shift_y(ahead_y[:, :half], 1), shift_y(back_y[:, half:], -1)]
        chunks += [group, ahead_y, back_y] + far_y
        counts += [len(away)] * 4
        halved += [False, False, False, True]
        steps += [(dy, dz) for dy in (0, -1, 1, 2) for dz in away]
    counts, halved = tuple(counts), tuple(halved)
    chunk_y = (my_y + jnp.array([dy for dy, _ in steps], jnp.int32)) % (YL * YH)
    chunk_z = (my_z + jnp.array([dz for _, dz in steps], jnp.int32)) % ZN
    chip = (chunk_y % YL * ZN + chunk_z) * YH + chunk_y // YL
    first_block = (chunk_y % YL * ZN + chunk_z) * CORES * YH + chunk_y // YL

    pool = exchange(pool, PLANE)
    pool, chunks[3:5], chunks[6:10] = lax.optimization_barrier((pool, chunks[3:5], chunks[6:10]))

    other_weight = swap(own_weight)

    chosen_rows = jnp.take(adapter_pool_rows, segment_adapters.reshape(-1), mode="clip")
    chosen = exchange(jnp.take(pool, chosen_rows, axis=0, mode="clip"), "grp")
    chosen = chosen.reshape(GRP, segs, depth, share)
    other_chosen = swap(chosen)
    by_core = (jnp.where(first, chosen, other_chosen), jnp.where(first, other_chosen, chosen))
    columns = []
    for part in by_core:
        part = part[:, :, rank:].reshape(YL, GRP // YL, segs, -1, CORES, YH, cols, share)
        part = jnp.transpose(part, (0, 1, 3, 5, 2, 6, 4, 7))
        part = part.reshape(SHARES // CORES, segs, cols, both)
        part = jnp.pad(part, ((0, 0), (0, 1), (0, SLOT - cols), (0, 0)))
        columns.append(part.reshape(SHARES // CORES, -1, both))
    columns = jnp.concatenate(columns, axis=1)
    own_factors, other_factors = chosen[:, :, :rank], other_chosen[:, :, :rank]

    bounds = jnp.cumsum(segment_tile_counts[0])
    positions = jnp.arange(tile_count, dtype=jnp.int32)
    tile_seg = jnp.sum((bounds[None, :] <= positions[:, None]).astype(jnp.int32), axis=1)
    tile_seg = lax.dynamic_slice_in_dim(tile_seg, core * (tile_count // CORES), tile_count // CORES)

    columns, own_factors, other_factors, own_weight, other_weight = lax.optimization_barrier(
        (columns, own_factors, other_factors, own_weight, other_weight)
    )

    own_columns = shrink(chunks, counts, halved, columns, chip, tile_seg, rows, both)
    own_columns = own_columns[:, :cols].astype(bf16)
    chips = SHARES // CORES
    shrunk = exchange(jnp.broadcast_to(own_columns[None], (chips, CORES, cols, rows)), CHIPS)
    shrunk = jnp.transpose(shrunk.reshape(YL * ZN, YH, CORES, cols, rows), (0, 2, 1, 3, 4))
    shrunk = shrunk.reshape(twice_rank, rows)

    frozen = frozen_matmul(
        chunks, counts, halved, own_weight, other_weight, first_block, rows, both
    )
    hidden = adapt(frozen, shrunk, own_factors, other_factors, tile_seg)

    other_rows = swap(hidden[1])
    return jnp.concatenate(
        [jnp.where(first, hidden[0], other_rows), jnp.where(first, other_rows, hidden[0])]
    )


def solution(mesh):
    fine = Mesh(mesh.devices.reshape(GRP, YL, ZN, CORES, YH), AXES)
    return jax.shard_map(
        per_device,
        mesh=fine,
        in_specs=(
            P("grp", PLANE),
            P(None, None, PLANE),
            P(PLANE, "grp", None),
            P(PLANE, "grp", None, None, None),
            P(),
            P("grp", None),
            P(),
        ),
        out_specs=P("grp", PLANE),
        check_vma=False,
    )
```

```python
import jax
import jax.numpy as jnp
from jax import lax
from jax.experimental import pallas as pl
from jax.experimental.pallas import tpu as pltpu
from jax.sharding import Mesh, PartitionSpec as P

TILE = 128
GRP = 4
YL, ZN, CORES, YH = 2, 8, 2, 2
AXES = ("grp", "ylo", "z", "core", "yhi")
PLANE = ("ylo", "z", "core", "yhi")
CHIPS = ("ylo", "z", "yhi")
SHARES = YL * ZN * CORES * YH
f32 = jnp.float32
bf16 = jnp.bfloat16

adapter_scale = 0.5

SLOT = 8
STEPS = 4


def shrink_kernel(tile_seg, tokens, columns, out, total):
    step = pl.program_id(0)
    part = lax.dot_general(
        columns[...], tokens[...], (((1,), (1,)), ((), ())), preferred_element_type=f32
    )

    @pl.when(step == 0)
    def _():
        total[...] = part

    @pl.when(step > 0)
    def _():
        total[...] += part

    @pl.when(step == pl.num_programs(0) - 1)
    def _():
        per = columns.shape[0] // CORES
        for c in range(CORES):
            for i in range(out.shape[2] // TILE):
                seg = tile_seg[i]
                at = slice(i * TILE, (i + 1) * TILE)
                pick = total[c * per : c * per + SLOT, at]
                for j in range(1, per // SLOT):
                    low = c * per + j * SLOT
                    pick = jnp.where(seg == j, total[low : low + SLOT, at], pick)
                out[c, :, at] = pick


def shrink(tokens, columns, tile_seg):
    count, width = tokens.shape
    slots = columns.shape[0]
    part = width // STEPS
    return pl.pallas_call(
        shrink_kernel,
        out_shape=jax.ShapeDtypeStruct((CORES, SLOT, count), f32),
        grid_spec=pltpu.PrefetchScalarGridSpec(
            num_scalar_prefetch=1,
            grid=(STEPS,),
            in_specs=[
                pl.BlockSpec((count, part), lambda k, seg: (0, k)),
                pl.BlockSpec((slots, part), lambda k, seg: (0, k)),
            ],
            out_specs=pl.BlockSpec((CORES, SLOT, count), lambda k, seg: (0, 0, 0)),
            scratch_shapes=[pltpu.VMEM((slots, count), f32)],
        ),
        compiler_params=pltpu.CompilerParams(
            dimension_semantics=("arbitrary",), vmem_limit_bytes=56 << 20
        ),
        name="shrink",
    )(tile_seg, tokens, columns)


def frozen_kernel(tokens, own, other, out):
    step = pl.program_id(0)
    for which, weight in enumerate((own, other)):
        part = jnp.dot(tokens[...], weight[...], preferred_element_type=f32)

        @pl.when(step == 0)
        def _():
            out[which] = part

        @pl.when(step > 0)
        def _():
            out[which] += part


def frozen_matmul(tokens, own, other):
    count, width = tokens.shape
    wide = own.shape[1]
    part = width // STEPS
    shape = (CORES, count, wide)
    weight = pl.BlockSpec((part, wide), lambda k: (k, 0))
    return pl.pallas_call(
        frozen_kernel,
        out_shape=jax.ShapeDtypeStruct(shape, f32),
        grid=(STEPS,),
        in_specs=[pl.BlockSpec((count, part), lambda k: (0, k)), weight, weight],
        out_specs=pl.BlockSpec(shape, lambda k: (0, 0, 0)),
        compiler_params=pltpu.CompilerParams(
            dimension_semantics=("arbitrary",), vmem_limit_bytes=56 << 20
        ),
        name="frozen",
    )(tokens, own, other)


def adapt_kernel(tile_seg, frozen, shrunk, own, other, out):
    parts, _, rank, _ = own.shape
    hidden = out.shape[2]
    low = lax.broadcasted_iota(jnp.int32, (TILE, rank), 1) < rank // 2
    seg = tile_seg[pl.program_id(0)]
    left = shrunk[...].astype(f32)
    gate_left = left[:rank].T.astype(bf16)
    up_left = left[rank:].T.astype(bf16)
    for which, factors in enumerate((own, other)):
        wide = jnp.concatenate([factors[m, seg] for m in range(parts)], axis=1)
        for_gate = jnp.dot(gate_left, wide, preferred_element_type=f32)
        for_up = jnp.dot(up_left, wide, preferred_element_type=f32)
        for a in range(parts // 2):
            even = slice(2 * a * rank, (2 * a + 1) * rank)
            odd = slice((2 * a + 1) * rank, (2 * a + 2) * rank)
            at = slice(a * rank, (a + 1) * rank)
            gate = jnp.where(low, for_gate[:, even], pltpu.roll(for_gate[:, odd], rank // 2, 1))
            up = jnp.where(low, pltpu.roll(for_up[:, even], rank // 2, 1), for_up[:, odd])
            gate = frozen[which, :, at] + adapter_scale * gate
            up = frozen[which, :, hidden + a * rank : hidden + (a + 1) * rank] + adapter_scale * up
            out[which, :, at] = (gate / (1.0 + jnp.exp(-gate)) * up).astype(bf16)


def adapt(frozen, shrunk, own, other, tile_seg):
    both, count, wide = frozen.shape
    whole = pl.BlockSpec(own.shape, lambda i, seg: (0, 0, 0, 0))
    return pl.pallas_call(
        adapt_kernel,
        out_shape=jax.ShapeDtypeStruct((both, count, wide // 2), bf16),
        grid_spec=pltpu.PrefetchScalarGridSpec(
            num_scalar_prefetch=1,
            grid=(count // TILE,),
            in_specs=[
                pl.BlockSpec((both, TILE, wide), lambda i, seg: (0, i, 0)),
                pl.BlockSpec((shrunk.shape[0], TILE), lambda i, seg: (0, i)),
                whole,
                whole,
            ],
            out_specs=pl.BlockSpec((both, TILE, wide // 2), lambda i, seg: (0, i, 0)),
        ),
        compiler_params=pltpu.CompilerParams(
            dimension_semantics=("arbitrary",), vmem_limit_bytes=56 << 20
        ),
        name="adapt",
    )(tile_seg, frozen, shrunk, own, other)


def exchange(x, axes):
    return lax.all_to_all(x, axes, split_axis=0, concat_axis=0, tiled=True)


def swap(x):
    return lax.ppermute(x, "core", [(0, 1), (1, 0)])


def per_device(
    tokens,
    gate_up_weight,
    down_factor_pool,
    up_factor_pool,
    segment_adapters,
    segment_tile_counts,
    adapter_pool_rows,
):
    core = lax.axis_index("core")
    first = core == 0
    token_count, share = tokens.shape
    tile_count = token_count // TILE
    width = gate_up_weight.shape[0]
    wide = 2 * gate_up_weight.shape[2]
    twice_rank = down_factor_pool.shape[2]
    rank = twice_rank // 2
    segs = segment_adapters.shape[1]
    rows = token_count // CORES

    kept = lax.dynamic_slice_in_dim(tokens, core * rows, rows, axis=0)
    given = swap(lax.dynamic_slice_in_dim(tokens, (1 - core) * rows, rows, axis=0))
    start = jnp.concatenate(
        [jnp.where(first, kept, given), jnp.where(first, given, kept)], axis=1
    )
    down_pool, start = lax.optimization_barrier((down_factor_pool[0], start))
    gathered = lax.all_gather(start, ("yhi", "ylo", "z"), axis=1, tiled=True)

    cols = twice_rank // SHARES
    depth = rank + share // 2
    down_pool = down_pool.T.reshape(SHARES, cols, -1, share)
    down_pool = jnp.transpose(down_pool, (0, 2, 1, 3)).reshape(SHARES, depth - rank, share)
    pool = jnp.concatenate([up_factor_pool.reshape(SHARES, rank, rank), down_pool], axis=1)
    pool = exchange(pool, PLANE)

    w = gate_up_weight.reshape(YL * ZN * CORES, YH, share, wide)
    own_weight = jnp.transpose(w, (1, 0, 2, 3)).reshape(width, wide)
    pool, own_weight = lax.optimization_barrier((pool, own_weight))
    other_weight = swap(own_weight)

    chosen_rows = jnp.take(adapter_pool_rows, segment_adapters.reshape(-1), mode="clip")
    chosen = exchange(jnp.take(pool, chosen_rows, axis=0, mode="clip"), "grp")
    chosen = chosen.reshape(GRP, segs, depth, share)
    other_chosen = swap(chosen)
    columns = []
    for part in (jnp.where(first, chosen, other_chosen), jnp.where(first, other_chosen, chosen)):
        part = part[:, :, rank:].reshape(YL, GRP // YL, segs, -1, CORES, YH, cols, share)
        part = jnp.transpose(part, (2, 6, 5, 0, 1, 3, 4, 7)).reshape(segs, cols, width)
        columns.append(jnp.pad(part, ((0, 1), (0, SLOT - cols), (0, 0))).reshape(-1, width))
    columns = jnp.concatenate(columns)
    own_factors, other_factors = chosen[:, :, :rank], other_chosen[:, :, :rank]

    bounds = jnp.cumsum(segment_tile_counts[0])
    positions = jnp.arange(tile_count, dtype=jnp.int32)
    tile_seg = jnp.sum((bounds[None, :] <= positions[:, None]).astype(jnp.int32), axis=1)
    tile_seg = lax.dynamic_slice_in_dim(tile_seg, core * (tile_count // CORES), tile_count // CORES)

    columns, own_factors, other_factors, other_weight = lax.optimization_barrier(
        (columns, own_factors, other_factors, other_weight)
    )

    own_columns = shrink(gathered, columns, tile_seg)[:, :cols].astype(bf16)
    chips = SHARES // CORES
    shrunk = exchange(jnp.broadcast_to(own_columns[None], (chips, CORES, cols, rows)), CHIPS)
    shrunk = jnp.transpose(shrunk.reshape(YL * ZN, YH, CORES, cols, rows), (0, 2, 1, 3, 4))
    shrunk = shrunk.reshape(twice_rank, rows)

    frozen = frozen_matmul(gathered, own_weight, other_weight)
    hidden = adapt(frozen, shrunk, own_factors, other_factors, tile_seg)

    other_rows = swap(hidden[1])
    return jnp.concatenate(
        [jnp.where(first, hidden[0], other_rows), jnp.where(first, other_rows, hidden[0])]
    )


def solution(mesh):
    fine = Mesh(mesh.devices.reshape(GRP, YL, ZN, CORES, YH), AXES)
    return jax.shard_map(
        per_device,
        mesh=fine,
        in_specs=(
            P("grp", PLANE),
            P(None, None, PLANE),
            P(PLANE, "grp", None),
            P(PLANE, "grp", None, None, None),
            P(),
            P("grp", None),
            P(),
        ),
        out_specs=P("grp", PLANE),
        check_vma=False,
    )
```

```python
import jax
import jax.numpy as jnp
from jax import lax
from jax.experimental import pallas as pl
from jax.experimental.pallas import tpu as pltpu
from jax.sharding import Mesh, PartitionSpec as P

TILE = 128
GRP = 4
YL, ZN, CORES, YH = 2, 8, 2, 2
AXES = ("grp", "ylo", "z", "core", "yhi")
PLANE = ("ylo", "z", "core", "yhi")
CHIPS = ("ylo", "z", "yhi")
SHARES = YL * ZN * CORES * YH
f32 = jnp.float32
bf16 = jnp.bfloat16

adapter_scale = 0.5

SLOT = 8
STEPS = 4


def shrink_kernel(tile_seg, tokens, columns, out, total):
    step = pl.program_id(0)
    block = jnp.concatenate([tokens[i] for i in range(tokens.shape[0])], axis=1)
    part = lax.dot_general(
        columns[...], block, (((1,), (1,)), ((), ())), preferred_element_type=f32
    )

    @pl.when(step == 0)
    def _():
        total[...] = part

    @pl.when(step > 0)
    def _():
        total[...] += part

    @pl.when(step == pl.num_programs(0) - 1)
    def _():
        per = columns.shape[0] // CORES
        for c in range(CORES):
            for i in range(out.shape[2] // TILE):
                seg = tile_seg[i]
                at = slice(i * TILE, (i + 1) * TILE)
                pick = total[c * per : c * per + SLOT, at]
                for j in range(1, per // SLOT):
                    low = c * per + j * SLOT
                    pick = jnp.where(seg == j, total[low : low + SLOT, at], pick)
                out[c, :, at] = pick


def shrink(tokens, columns, tile_seg):
    chips, count, both = tokens.shape
    slots, width = columns.shape
    part = width // STEPS
    return pl.pallas_call(
        shrink_kernel,
        out_shape=jax.ShapeDtypeStruct((CORES, SLOT, count), f32),
        grid_spec=pltpu.PrefetchScalarGridSpec(
            num_scalar_prefetch=1,
            grid=(STEPS,),
            in_specs=[
                pl.BlockSpec((chips // STEPS, count, both), lambda k, seg: (k, 0, 0)),
                pl.BlockSpec((slots, part), lambda k, seg: (0, k)),
            ],
            out_specs=pl.BlockSpec((CORES, SLOT, count), lambda k, seg: (0, 0, 0)),
            scratch_shapes=[pltpu.VMEM((slots, count), f32)],
        ),
        compiler_params=pltpu.CompilerParams(
            dimension_semantics=("arbitrary",), vmem_limit_bytes=56 << 20
        ),
        name="shrink",
    )(tile_seg, tokens, columns)


def frozen_kernel(tokens, own, other, out):
    step = pl.program_id(0)
    block = jnp.concatenate([tokens[i] for i in range(tokens.shape[0])], axis=1)
    for which, weight in enumerate((own, other)):
        part = jnp.dot(block, weight[...], preferred_element_type=f32)

        @pl.when(step == 0)
        def _():
            out[which] = part

        @pl.when(step > 0)
        def _():
            out[which] += part


def frozen_matmul(tokens, own, other):
    chips, count, both = tokens.shape
    width, wide = own.shape
    part = width // STEPS
    shape = (CORES, count, wide)
    weight = pl.BlockSpec((part, wide), lambda k: (k, 0))
    return pl.pallas_call(
        frozen_kernel,
        out_shape=jax.ShapeDtypeStruct(shape, f32),
        grid=(STEPS,),
        in_specs=[
            pl.BlockSpec((chips // STEPS, count, both), lambda k: (k, 0, 0)),
            weight,
            weight,
        ],
        out_specs=pl.BlockSpec(shape, lambda k: (0, 0, 0)),
        compiler_params=pltpu.CompilerParams(
            dimension_semantics=("arbitrary",), vmem_limit_bytes=56 << 20
        ),
        name="frozen",
    )(tokens, own, other)


def adapt_kernel(tile_seg, frozen, shrunk, own, other, own_out, other_out):
    parts, _, rank, _ = own.shape
    hidden = own_out.shape[1]
    low = lax.broadcasted_iota(jnp.int32, (TILE, rank), 1) < rank // 2
    seg = tile_seg[pl.program_id(0)]
    left = shrunk[...].astype(f32)
    gate_left = left[:rank].T.astype(bf16)
    up_left = left[rank:].T.astype(bf16)
    for which, (factors, out) in enumerate(((own, own_out), (other, other_out))):
        wide = jnp.concatenate([factors[m, seg] for m in range(parts)], axis=1)
        for_gate = jnp.dot(gate_left, wide, preferred_element_type=f32)
        for_up = jnp.dot(up_left, wide, preferred_element_type=f32)
        for a in range(parts // 2):
            even = slice(2 * a * rank, (2 * a + 1) * rank)
            odd = slice((2 * a + 1) * rank, (2 * a + 2) * rank)
            at = slice(a * rank, (a + 1) * rank)
            gate = jnp.where(low, for_gate[:, even], pltpu.roll(for_gate[:, odd], rank // 2, 1))
            up = jnp.where(low, pltpu.roll(for_up[:, even], rank // 2, 1), for_up[:, odd])
            gate = frozen[which, :, at] + adapter_scale * gate
            up = frozen[which, :, hidden + a * rank : hidden + (a + 1) * rank] + adapter_scale * up
            out[:, at] = (gate / (1.0 + jnp.exp(-gate)) * up).astype(bf16)


def adapt(frozen, shrunk, own, other, tile_seg):
    both, count, wide = frozen.shape
    whole = pl.BlockSpec(own.shape, lambda i, seg: (0, 0, 0, 0))
    return pl.pallas_call(
        adapt_kernel,
        out_shape=[jax.ShapeDtypeStruct((count, wide // 2), bf16)] * both,
        grid_spec=pltpu.PrefetchScalarGridSpec(
            num_scalar_prefetch=1,
            grid=(count // TILE,),
            in_specs=[
                pl.BlockSpec((both, TILE, wide), lambda i, seg: (0, i, 0)),
                pl.BlockSpec((shrunk.shape[0], TILE), lambda i, seg: (0, i)),
                whole,
                whole,
            ],
            out_specs=[pl.BlockSpec((TILE, wide // 2), lambda i, seg: (i, 0))] * both,
        ),
        compiler_params=pltpu.CompilerParams(
            dimension_semantics=("arbitrary",), vmem_limit_bytes=56 << 20
        ),
        name="adapt",
    )(tile_seg, frozen, shrunk, own, other)


def exchange(x, axes):
    return lax.all_to_all(x, axes, split_axis=0, concat_axis=0, tiled=True)


def swap(x):
    return lax.ppermute(x, "core", [(0, 1), (1, 0)])


def per_device(
    tokens,
    gate_up_weight,
    down_factor_pool,
    up_factor_pool,
    segment_adapters,
    segment_tile_counts,
    adapter_pool_rows,
):
    core = lax.axis_index("core")
    first = core == 0
    token_count, share = tokens.shape
    tile_count = token_count // TILE
    width = gate_up_weight.shape[0]
    wide = 2 * gate_up_weight.shape[2]
    twice_rank = down_factor_pool.shape[2]
    rank = twice_rank // 2
    segs = segment_adapters.shape[1]
    rows = token_count // CORES

    kept = lax.dynamic_slice_in_dim(tokens, core * rows, rows, axis=0)
    given = swap(lax.dynamic_slice_in_dim(tokens, (1 - core) * rows, rows, axis=0))
    start = jnp.concatenate(
        [jnp.where(first, kept, given), jnp.where(first, given, kept)], axis=1
    )
    down_pool, start = lax.optimization_barrier((down_factor_pool[0], start))
    gathered = lax.all_gather(start, ("yhi", "ylo", "z"))
    gathered = gathered.reshape(SHARES // CORES, rows, CORES * share)

    cols = twice_rank // SHARES
    depth = rank + share // 2
    down_pool = down_pool.T.reshape(SHARES, cols, -1, share)
    down_pool = jnp.transpose(down_pool, (0, 2, 1, 3)).reshape(SHARES, depth - rank, share)
    pool = jnp.concatenate([up_factor_pool.reshape(SHARES, rank, rank), down_pool], axis=1)
    pool = exchange(pool, PLANE)

    w = gate_up_weight.reshape(YL * ZN * CORES, YH, share, wide)
    own_weight = jnp.transpose(w, (1, 0, 2, 3)).reshape(width, wide)
    pool, own_weight = lax.optimization_barrier((pool, own_weight))
    other_weight = swap(own_weight)

    chosen_rows = jnp.take(adapter_pool_rows, segment_adapters.reshape(-1), mode="clip")
    chosen = exchange(jnp.take(pool, chosen_rows, axis=0, mode="clip"), "grp")
    chosen = chosen.reshape(GRP, segs, depth, share)
    other_chosen = swap(chosen)
    columns = []
    for part in (jnp.where(first, chosen, other_chosen), jnp.where(first, other_chosen, chosen)):
        part = part[:, :, rank:].reshape(YL, GRP // YL, segs, -1, CORES, YH, cols, share)
        part = jnp.transpose(part, (2, 6, 5, 0, 1, 3, 4, 7)).reshape(segs, cols, width)
        columns.append(jnp.pad(part, ((0, 1), (0, SLOT - cols), (0, 0))).reshape(-1, width))
    columns = jnp.concatenate(columns)
    own_factors, other_factors = chosen[:, :, :rank], other_chosen[:, :, :rank]

    bounds = jnp.cumsum(segment_tile_counts[0])
    positions = jnp.arange(tile_count, dtype=jnp.int32)
    tile_seg = jnp.sum((bounds[None, :] <= positions[:, None]).astype(jnp.int32), axis=1)
    tile_seg = lax.dynamic_slice_in_dim(tile_seg, core * (tile_count // CORES), tile_count // CORES)

    columns, own_factors, other_factors, other_weight = lax.optimization_barrier(
        (columns, own_factors, other_factors, other_weight)
    )

    own_columns = shrink(gathered, columns, tile_seg)[:, :cols].astype(bf16)
    chips = SHARES // CORES
    shrunk = exchange(jnp.broadcast_to(own_columns[None], (chips, CORES, cols, rows)), CHIPS)
    shrunk = jnp.transpose(shrunk.reshape(YL * ZN, YH, CORES, cols, rows), (0, 2, 1, 3, 4))
    shrunk = shrunk.reshape(twice_rank, rows)

    frozen = frozen_matmul(gathered, own_weight, other_weight)
    own_rows, for_other = adapt(frozen, shrunk, own_factors, other_factors, tile_seg)

    hidden = jnp.zeros((token_count, wide // 2), bf16)
    hidden = lax.dynamic_update_slice_in_dim(hidden, own_rows, core * rows, axis=0)
    return lax.dynamic_update_slice_in_dim(hidden, swap(for_other), (1 - core) * rows, axis=0)


def solution(mesh):
    fine = Mesh(mesh.devices.reshape(GRP, YL, ZN, CORES, YH), AXES)
    return jax.shard_map(
        per_device,
        mesh=fine,
        in_specs=(
            P("grp", PLANE),
            P(None, None, PLANE),
            P(PLANE, "grp", None),
            P(PLANE, "grp", None, None, None),
            P(),
            P("grp", None),
            P(),
        ),
        out_specs=P("grp", PLANE),
        check_vma=False,
    )
```

```python
import jax
import jax.numpy as jnp
from jax import lax
from jax.experimental import pallas as pl
from jax.experimental.pallas import tpu as pltpu
from jax.sharding import Mesh, PartitionSpec as P

TILE = 128
GRP = 4
YL, ZN, CORES, YH = 2, 8, 2, 2
AXES = ("grp", "ylo", "z", "core", "yhi")
PLANE = ("ylo", "z", "core", "yhi")
CHIPS = ("ylo", "z", "yhi")
SHARES = YL * ZN * CORES * YH
f32 = jnp.float32
bf16 = jnp.bfloat16

adapter_scale = 0.5

SLOT = 8
STEPS = 4
HALVES = 2


def shrink_kernel(tile_seg, tokens, columns, out, total):
    step = pl.program_id(0)
    block = jnp.concatenate([tokens[i] for i in range(tokens.shape[0])], axis=1)
    part = lax.dot_general(
        columns[...], block, (((1,), (1,)), ((), ())), preferred_element_type=f32
    )

    @pl.when(step == 0)
    def _():
        total[...] = part

    @pl.when(step > 0)
    def _():
        total[...] += part

    @pl.when(step == pl.num_programs(0) - 1)
    def _():
        per = columns.shape[0] // CORES
        for c in range(CORES):
            for i in range(out.shape[3] // TILE):
                seg = tile_seg[i]
                at = slice(i * TILE, (i + 1) * TILE)
                pick = total[c * per : c * per + SLOT, at]
                for j in range(1, per // SLOT):
                    low = c * per + j * SLOT
                    pick = jnp.where(seg == j, total[low : low + SLOT, at], pick)
                pick = pick[: out.shape[2]].astype(bf16)
                for chip in range(out.shape[0]):
                    out[chip, c, :, at] = pick


def shrink(tokens, columns, tile_seg, cols):
    chips, count, both = tokens.shape
    slots, width = columns.shape
    part = width // HALVES
    return pl.pallas_call(
        shrink_kernel,
        out_shape=jax.ShapeDtypeStruct((chips, CORES, cols, count), bf16),
        grid_spec=pltpu.PrefetchScalarGridSpec(
            num_scalar_prefetch=1,
            grid=(HALVES,),
            in_specs=[
                pl.BlockSpec((chips // HALVES, count, both), lambda k, seg: (k, 0, 0)),
                pl.BlockSpec((slots, part), lambda k, seg: (0, k)),
            ],
            out_specs=pl.BlockSpec((chips, CORES, cols, count), lambda k, seg: (0, 0, 0, 0)),
            scratch_shapes=[pltpu.VMEM((slots, count), f32)],
        ),
        compiler_params=pltpu.CompilerParams(
            dimension_semantics=("arbitrary",), vmem_limit_bytes=56 << 20
        ),
        name="shrink",
    )(tile_seg, tokens, columns)


def frozen_kernel(tokens, own, other, out):
    step = pl.program_id(0)
    block = jnp.concatenate([tokens[i] for i in range(tokens.shape[0])], axis=1)
    for which, weight in enumerate((own, other)):
        part = jnp.dot(block, weight[...], preferred_element_type=f32)

        @pl.when(step == 0)
        def _():
            out[which] = part

        @pl.when(step > 0)
        def _():
            out[which] += part


def frozen_matmul(tokens, own, other):
    chips, count, both = tokens.shape
    width, wide = own.shape
    part = width // STEPS
    shape = (CORES, count, wide)
    weight = pl.BlockSpec((part, wide), lambda k: (k, 0))
    return pl.pallas_call(
        frozen_kernel,
        out_shape=jax.ShapeDtypeStruct(shape, f32),
        grid=(STEPS,),
        in_specs=[
            pl.BlockSpec((chips // STEPS, count, both), lambda k: (k, 0, 0)),
            weight,
            weight,
        ],
        out_specs=pl.BlockSpec(shape, lambda k: (0, 0, 0)),
        compiler_params=pltpu.CompilerParams(
            dimension_semantics=("arbitrary",), vmem_limit_bytes=56 << 20
        ),
        name="frozen",
    )(tokens, own, other)


def adapt_kernel(tile_seg, frozen, shrunk, own, other, own_out, other_out):
    parts, _, rank, _ = own.shape
    hidden = own_out.shape[1]
    tiles = own_out.shape[0] // TILE
    low = lax.broadcasted_iota(jnp.int32, (TILE, rank), 1) < rank // 2
    for t in range(tiles):
        seg = tile_seg[pl.program_id(0) * tiles + t]
        row = slice(t * TILE, (t + 1) * TILE)
        left = shrunk[:, row].astype(f32)
        gate_left = left[:rank].T.astype(bf16)
        up_left = left[rank:].T.astype(bf16)
        for which, (factors, out) in enumerate(((own, own_out), (other, other_out))):
            wide = jnp.concatenate([factors[m, seg] for m in range(parts)], axis=1)
            for_gate = jnp.dot(gate_left, wide, preferred_element_type=f32)
            for_up = jnp.dot(up_left, wide, preferred_element_type=f32)
            for a in range(parts // 2):
                even = slice(2 * a * rank, (2 * a + 1) * rank)
                odd = slice((2 * a + 1) * rank, (2 * a + 2) * rank)
                at = slice(a * rank, (a + 1) * rank)
                gate = jnp.where(
                    low, for_gate[:, even], pltpu.roll(for_gate[:, odd], rank // 2, 1)
                )
                up = jnp.where(low, pltpu.roll(for_up[:, even], rank // 2, 1), for_up[:, odd])
                gate = frozen[which, row, at] + adapter_scale * gate
                up = (
                    frozen[which, row, hidden + a * rank : hidden + (a + 1) * rank]
                    + adapter_scale * up
                )
                out[row, at] = (gate / (1.0 + jnp.exp(-gate)) * up).astype(bf16)


def adapt(frozen, shrunk, own, other, tile_seg):
    both, count, wide = frozen.shape
    rows = count // HALVES
    whole = pl.BlockSpec(own.shape, lambda i, seg: (0, 0, 0, 0))
    return pl.pallas_call(
        adapt_kernel,
        out_shape=[jax.ShapeDtypeStruct((count, wide // 2), bf16)] * both,
        grid_spec=pltpu.PrefetchScalarGridSpec(
            num_scalar_prefetch=1,
            grid=(HALVES,),
            in_specs=[
                pl.BlockSpec((both, rows, wide), lambda i, seg: (0, i, 0)),
                pl.BlockSpec((shrunk.shape[0], rows), lambda i, seg: (0, i)),
                whole,
                whole,
            ],
            out_specs=[pl.BlockSpec((rows, wide // 2), lambda i, seg: (i, 0))] * both,
        ),
        compiler_params=pltpu.CompilerParams(
            dimension_semantics=("arbitrary",), vmem_limit_bytes=56 << 20
        ),
        name="adapt",
    )(tile_seg, frozen, shrunk, own, other)


def exchange(x, axes):
    return lax.all_to_all(x, axes, split_axis=0, concat_axis=0, tiled=True)


def swap(x):
    return lax.ppermute(x, "core", [(0, 1), (1, 0)])


def per_device(
    tokens,
    gate_up_weight,
    down_factor_pool,
    up_factor_pool,
    segment_adapters,
    segment_tile_counts,
    adapter_pool_rows,
):
    core = lax.axis_index("core")
    first = core == 0
    token_count, share = tokens.shape
    tile_count = token_count // TILE
    width = gate_up_weight.shape[0]
    wide = 2 * gate_up_weight.shape[2]
    twice_rank = down_factor_pool.shape[2]
    rank = twice_rank // 2
    segs = segment_adapters.shape[1]
    rows = token_count // CORES

    kept = lax.dynamic_slice_in_dim(tokens, core * rows, rows, axis=0)
    given = swap(lax.dynamic_slice_in_dim(tokens, (1 - core) * rows, rows, axis=0))
    start = jnp.concatenate(
        [jnp.where(first, kept, given), jnp.where(first, given, kept)], axis=1
    )
    down_pool, start = lax.optimization_barrier((down_factor_pool[0], start))
    gathered = lax.all_gather(start, ("yhi", "ylo", "z"))
    gathered = gathered.reshape(SHARES // CORES, rows, CORES * share)

    cols = twice_rank // SHARES
    depth = rank + share // 2
    down_pool = down_pool.T.reshape(SHARES, cols, -1, share)
    down_pool = jnp.transpose(down_pool, (0, 2, 1, 3)).reshape(SHARES, depth - rank, share)
    pool = jnp.concatenate([up_factor_pool.reshape(SHARES, rank, rank), down_pool], axis=1)
    pool = exchange(pool, PLANE)

    w = gate_up_weight.reshape(YL * ZN * CORES, YH, share, wide)
    own_weight = jnp.transpose(w, (1, 0, 2, 3)).reshape(width, wide)
    pool, own_weight = lax.optimization_barrier((pool, own_weight))
    other_weight = swap(own_weight)

    chosen_rows = jnp.take(adapter_pool_rows, segment_adapters.reshape(-1), mode="clip")
    chosen = exchange(jnp.take(pool, chosen_rows, axis=0, mode="clip"), "grp")
    chosen = chosen.reshape(GRP, segs, depth, share)
    other_chosen = swap(chosen)
    columns = []
    for part in (jnp.where(first, chosen, other_chosen), jnp.where(first, other_chosen, chosen)):
        part = part[:, :, rank:].reshape(YL, GRP // YL, segs, -1, CORES, YH, cols, share)
        part = jnp.transpose(part, (2, 6, 5, 0, 1, 3, 4, 7)).reshape(segs, cols, width)
        columns.append(jnp.pad(part, ((0, 1), (0, SLOT - cols), (0, 0))).reshape(-1, width))
    columns = jnp.concatenate(columns)
    own_factors, other_factors = chosen[:, :, :rank], other_chosen[:, :, :rank]

    bounds = jnp.cumsum(segment_tile_counts[0])
    positions = jnp.arange(tile_count, dtype=jnp.int32)
    tile_seg = jnp.sum((bounds[None, :] <= positions[:, None]).astype(jnp.int32), axis=1)
    tile_seg = lax.dynamic_slice_in_dim(tile_seg, core * (tile_count // CORES), tile_count // CORES)

    columns, own_factors, other_factors, other_weight = lax.optimization_barrier(
        (columns, own_factors, other_factors, other_weight)
    )

    shrunk = exchange(shrink(gathered, columns, tile_seg, cols), CHIPS)
    shrunk = jnp.transpose(shrunk.reshape(YL * ZN, YH, CORES, cols, rows), (0, 2, 1, 3, 4))
    shrunk = shrunk.reshape(twice_rank, rows)

    frozen = frozen_matmul(gathered, own_weight, other_weight)
    own_rows, for_other = adapt(frozen, shrunk, own_factors, other_factors, tile_seg)

    hidden = jnp.zeros((token_count, wide // 2), bf16)
    hidden = lax.dynamic_update_slice_in_dim(hidden, own_rows, core * rows, axis=0)
    return lax.dynamic_update_slice_in_dim(hidden, swap(for_other), (1 - core) * rows, axis=0)


def solution(mesh):
    fine = Mesh(mesh.devices.reshape(GRP, YL, ZN, CORES, YH), AXES)
    return jax.shard_map(
        per_device,
        mesh=fine,
        in_specs=(
            P("grp", PLANE),
            P(None, None, PLANE),
            P(PLANE, "grp", None),
            P(PLANE, "grp", None, None, None),
            P(),
            P("grp", None),
            P(),
        ),
        out_specs=P("grp", PLANE),
        check_vma=False,
    )
```

```python
import jax
import jax.numpy as jnp
from jax import lax
from jax.experimental import pallas as pl
from jax.experimental.pallas import tpu as pltpu
from jax.sharding import Mesh, PartitionSpec as P

TILE = 128
GRP = 4
YL, ZN, CORES, YH = 2, 8, 2, 2
AXES = ("grp", "ylo", "z", "core", "yhi")
PLANE = ("ylo", "z", "core", "yhi")
CHIPS = ("ylo", "z", "yhi")
SHARES = YL * ZN * CORES * YH
f32 = jnp.float32
bf16 = jnp.bfloat16

adapter_scale = 0.5

SLOT = 8
STEPS = 4
HALVES = 2


def shrink_kernel(tile_seg, tokens, columns, out, total):
    step = pl.program_id(0)
    block = jnp.concatenate([tokens[i] for i in range(tokens.shape[0])], axis=1)
    part = lax.dot_general(
        columns[...], block, (((1,), (1,)), ((), ())), preferred_element_type=f32
    )

    @pl.when(step == 0)
    def _():
        total[...] = part

    @pl.when(step > 0)
    def _():
        total[...] += part

    @pl.when(step == pl.num_programs(0) - 1)
    def _():
        per = columns.shape[0] // CORES
        for c in range(CORES):
            for i in range(out.shape[3] // TILE):
                seg = tile_seg[i]
                at = slice(i * TILE, (i + 1) * TILE)
                pick = total[c * per : c * per + SLOT, at]
                for j in range(1, per // SLOT):
                    low = c * per + j * SLOT
                    pick = jnp.where(seg == j, total[low : low + SLOT, at], pick)
                pick = pick[: out.shape[2]].astype(bf16)
                for chip in range(out.shape[0]):
                    out[chip, c, :, at] = pick


def shrink(tokens, columns, tile_seg, cols):
    chips, count, both = tokens.shape
    slots, width = columns.shape
    part = width // HALVES
    return pl.pallas_call(
        shrink_kernel,
        out_shape=jax.ShapeDtypeStruct((chips, CORES, cols, count), bf16),
        grid_spec=pltpu.PrefetchScalarGridSpec(
            num_scalar_prefetch=1,
            grid=(HALVES,),
            in_specs=[
                pl.BlockSpec((chips // HALVES, count, both), lambda k, seg: (k, 0, 0)),
                pl.BlockSpec((slots, part), lambda k, seg: (0, k)),
            ],
            out_specs=pl.BlockSpec((chips, CORES, cols, count), lambda k, seg: (0, 0, 0, 0)),
            scratch_shapes=[pltpu.VMEM((slots, count), f32)],
        ),
        compiler_params=pltpu.CompilerParams(
            dimension_semantics=("arbitrary",), vmem_limit_bytes=56 << 20
        ),
        name="shrink",
    )(tile_seg, tokens, columns)


def frozen_kernel(tokens, own, other, out):
    step = pl.program_id(0)
    block = jnp.concatenate([tokens[i] for i in range(tokens.shape[0])], axis=1)
    for which, weight in enumerate((own, other)):
        part = jnp.dot(block, weight[...], preferred_element_type=f32)

        @pl.when(step == 0)
        def _():
            out[which] = part

        @pl.when(step > 0)
        def _():
            out[which] += part


def frozen_matmul(tokens, own, other):
    chips, count, both = tokens.shape
    width, wide = own.shape
    part = width // STEPS
    shape = (CORES, count, wide)
    weight = pl.BlockSpec((part, wide), lambda k: (k, 0))
    return pl.pallas_call(
        frozen_kernel,
        out_shape=jax.ShapeDtypeStruct(shape, f32),
        grid=(STEPS,),
        in_specs=[
            pl.BlockSpec((chips // STEPS, count, both), lambda k: (k, 0, 0)),
            weight,
            weight,
        ],
        out_specs=pl.BlockSpec(shape, lambda k: (0, 0, 0)),
        compiler_params=pltpu.CompilerParams(
            dimension_semantics=("arbitrary",), vmem_limit_bytes=56 << 20
        ),
        name="frozen",
    )(tokens, own, other)


def adapt_kernel(tile_seg, place, frozen, shrunk, own, other, own_out, other_out):
    parts, _, rank, _ = own.shape
    hidden = own_out.shape[1]
    tiles = own_out.shape[0] // TILE
    low = lax.broadcasted_iota(jnp.int32, (TILE, rank), 1) < rank // 2
    for t in range(tiles):
        seg = tile_seg[pl.program_id(0) * tiles + t]
        row = slice(t * TILE, (t + 1) * TILE)
        left = shrunk[:, row].astype(f32)
        gate_left = left[:rank].T.astype(bf16)
        up_left = left[rank:].T.astype(bf16)
        for which, (factors, out) in enumerate(((own, own_out), (other, other_out))):
            wide = jnp.concatenate([factors[m, seg] for m in range(parts)], axis=1)
            for_gate = jnp.dot(gate_left, wide, preferred_element_type=f32)
            for_up = jnp.dot(up_left, wide, preferred_element_type=f32)
            for a in range(parts // 2):
                even = slice(2 * a * rank, (2 * a + 1) * rank)
                odd = slice((2 * a + 1) * rank, (2 * a + 2) * rank)
                at = slice(a * rank, (a + 1) * rank)
                gate = jnp.where(
                    low, for_gate[:, even], pltpu.roll(for_gate[:, odd], rank // 2, 1)
                )
                up = jnp.where(low, pltpu.roll(for_up[:, even], rank // 2, 1), for_up[:, odd])
                gate = frozen[which, row, at] + adapter_scale * gate
                up = (
                    frozen[which, row, hidden + a * rank : hidden + (a + 1) * rank]
                    + adapter_scale * up
                )
                out[row, at] = (gate / (1.0 + jnp.exp(-gate)) * up).astype(bf16)


def adapt(frozen, shrunk, own, other, tile_seg, core):
    both, count, wide = frozen.shape
    rows = count // HALVES
    whole = pl.BlockSpec(own.shape, lambda i, seg, at: (0, 0, 0, 0))
    return pl.pallas_call(
        adapt_kernel,
        out_shape=[
            jax.ShapeDtypeStruct((CORES * count, wide // 2), bf16),
            jax.ShapeDtypeStruct((count, wide // 2), bf16),
        ],
        grid_spec=pltpu.PrefetchScalarGridSpec(
            num_scalar_prefetch=2,
            grid=(HALVES,),
            in_specs=[
                pl.BlockSpec((both, rows, wide), lambda i, seg, at: (0, i, 0)),
                pl.BlockSpec((shrunk.shape[0], rows), lambda i, seg, at: (0, i)),
                whole,
                whole,
            ],
            out_specs=[
                pl.BlockSpec((rows, wide // 2), lambda i, seg, at: (at[0] + i, 0)),
                pl.BlockSpec((rows, wide // 2), lambda i, seg, at: (i, 0)),
            ],
        ),
        compiler_params=pltpu.CompilerParams(
            dimension_semantics=("arbitrary",), vmem_limit_bytes=56 << 20
        ),
        name="adapt",
    )(tile_seg, (core * HALVES).reshape(1), frozen, shrunk, own, other)


def exchange(x, axes):
    return lax.all_to_all(x, axes, split_axis=0, concat_axis=0, tiled=True)


def swap(x):
    return lax.ppermute(x, "core", [(0, 1), (1, 0)])


def per_device(
    tokens,
    gate_up_weight,
    down_factor_pool,
    up_factor_pool,
    segment_adapters,
    segment_tile_counts,
    adapter_pool_rows,
):
    core = lax.axis_index("core")
    first = core == 0
    token_count, share = tokens.shape
    tile_count = token_count // TILE
    width = gate_up_weight.shape[0]
    wide = 2 * gate_up_weight.shape[2]
    twice_rank = down_factor_pool.shape[2]
    rank = twice_rank // 2
    segs = segment_adapters.shape[1]
    rows = token_count // CORES

    kept = lax.dynamic_slice_in_dim(tokens, core * rows, rows, axis=0)
    given = swap(lax.dynamic_slice_in_dim(tokens, (1 - core) * rows, rows, axis=0))
    start = jnp.where(
        first,
        jnp.concatenate([kept, given], axis=1),
        jnp.concatenate([given, kept], axis=1),
    )
    down_pool, start = lax.optimization_barrier((down_factor_pool[0], start))
    gathered = lax.all_gather(start, ("yhi", "ylo", "z"))
    gathered = gathered.reshape(SHARES // CORES, rows, CORES * share)

    cols = twice_rank // SHARES
    depth = rank + share // 2
    down_pool = down_pool.T.reshape(SHARES, cols, -1, share)
    down_pool = jnp.transpose(down_pool, (0, 2, 1, 3)).reshape(SHARES, depth - rank, share)
    pool = jnp.concatenate([up_factor_pool.reshape(SHARES, rank, rank), down_pool], axis=1)
    pool = exchange(pool, PLANE)

    w = gate_up_weight.reshape(YL * ZN * CORES, YH, share, wide)
    own_weight = jnp.transpose(w, (1, 0, 2, 3)).reshape(width, wide)
    pool, own_weight = lax.optimization_barrier((pool, own_weight))
    other_weight = swap(own_weight)

    chosen_rows = jnp.take(adapter_pool_rows, segment_adapters.reshape(-1), mode="clip")
    chosen = exchange(jnp.take(pool, chosen_rows, axis=0, mode="clip"), "grp")
    chosen = chosen.reshape(GRP, segs, depth, share)
    other_chosen = swap(chosen)
    columns = []
    for part in (jnp.where(first, chosen, other_chosen), jnp.where(first, other_chosen, chosen)):
        part = part[:, :, rank:].reshape(YL, GRP // YL, segs, -1, CORES, YH, cols, share)
        part = jnp.transpose(part, (2, 6, 5, 0, 1, 3, 4, 7)).reshape(segs, cols, width)
        columns.append(jnp.pad(part, ((0, 1), (0, SLOT - cols), (0, 0))).reshape(-1, width))
    columns = jnp.concatenate(columns)
    own_factors, other_factors = chosen[:, :, :rank], other_chosen[:, :, :rank]

    bounds = jnp.cumsum(segment_tile_counts[0])
    positions = jnp.arange(tile_count, dtype=jnp.int32)
    tile_seg = jnp.sum((bounds[None, :] <= positions[:, None]).astype(jnp.int32), axis=1)
    tile_seg = lax.dynamic_slice_in_dim(tile_seg, core * (tile_count // CORES), tile_count // CORES)

    columns, own_factors, other_factors, other_weight = lax.optimization_barrier(
        (columns, own_factors, other_factors, other_weight)
    )

    shrunk = exchange(shrink(gathered, columns, tile_seg, cols), CHIPS)
    shrunk = jnp.transpose(shrunk.reshape(YL * ZN, YH, CORES, cols, rows), (0, 2, 1, 3, 4))
    shrunk = shrunk.reshape(twice_rank, rows)

    frozen = frozen_matmul(gathered, own_weight, other_weight)
    hidden, for_other = adapt(frozen, shrunk, own_factors, other_factors, tile_seg, core)
    return lax.dynamic_update_slice_in_dim(hidden, swap(for_other), (1 - core) * rows, axis=0)


def solution(mesh):
    fine = Mesh(mesh.devices.reshape(GRP, YL, ZN, CORES, YH), AXES)
    return jax.shard_map(
        per_device,
        mesh=fine,
        in_specs=(
            P("grp", PLANE),
            P(None, None, PLANE),
            P(PLANE, "grp", None),
            P(PLANE, "grp", None, None, None),
            P(),
            P("grp", None),
            P(),
        ),
        out_specs=P("grp", PLANE),
        check_vma=False,
    )
```

```python
import jax
import jax.numpy as jnp
from jax import lax
from jax.experimental import pallas as pl
from jax.experimental.pallas import tpu as pltpu
from jax.sharding import Mesh, PartitionSpec as P

TILE = 128
GRP = 4
YL, ZN, CORES, YH = 2, 8, 2, 2
AXES = ("grp", "ylo", "z", "core", "yhi")
PLANE = ("ylo", "z", "core", "yhi")
CHIPS = ("ylo", "z", "yhi")
SHARES = YL * ZN * CORES * YH
f32 = jnp.float32
bf16 = jnp.bfloat16

adapter_scale = 0.5

SLOT = 8
TURNS = 8
DEEP = 4
HALVES = 2


def shrink_kernel(tile_seg, tokens, columns, out, total):
    step = pl.program_id(0)
    block = jnp.concatenate([tokens[i] for i in range(tokens.shape[0])], axis=1)
    part = lax.dot_general(
        columns[...], block, (((1,), (1,)), ((), ())), preferred_element_type=f32
    )

    @pl.when(step == 0)
    def _():
        total[...] = part

    @pl.when(step > 0)
    def _():
        total[...] += part

    @pl.when(step == pl.num_programs(0) - 1)
    def _():
        per = columns.shape[0] // CORES
        for c in range(CORES):
            for i in range(out.shape[3] // TILE):
                seg = tile_seg[i]
                at = slice(i * TILE, (i + 1) * TILE)
                pick = total[c * per : c * per + SLOT, at]
                for j in range(1, per // SLOT):
                    low = c * per + j * SLOT
                    pick = jnp.where(seg == j, total[low : low + SLOT, at], pick)
                pick = pick[: out.shape[2]].astype(bf16)
                for chip in range(out.shape[0]):
                    out[chip, c, :, at] = pick


def shrink(tokens, columns, tile_seg, cols):
    chips, count, both = tokens.shape
    slots, width = columns.shape
    part = width // HALVES
    return pl.pallas_call(
        shrink_kernel,
        out_shape=jax.ShapeDtypeStruct((chips, CORES, cols, count), bf16),
        grid_spec=pltpu.PrefetchScalarGridSpec(
            num_scalar_prefetch=1,
            grid=(HALVES,),
            in_specs=[
                pl.BlockSpec((chips // HALVES, count, both), lambda k, seg: (k, 0, 0)),
                pl.BlockSpec((slots, part), lambda k, seg: (0, k)),
            ],
            out_specs=pl.BlockSpec((chips, CORES, cols, count), lambda k, seg: (0, 0, 0, 0)),
            scratch_shapes=[pltpu.VMEM((slots, count), f32)],
        ),
        compiler_params=pltpu.CompilerParams(
            dimension_semantics=("arbitrary",), vmem_limit_bytes=56 << 20
        ),
        name="shrink",
    )(tile_seg, tokens, columns)


def frozen_kernel(tokens, own, other, out, block, weights, sems):
    turns = tokens.shape[0] // block.shape[1]
    deep, chips, count, both = block.shape
    part = chips * both

    def copies(k):
        slot = k % deep
        pairs = [(tokens.at[pl.ds(k * chips, chips)], block.at[slot])]
        for which, weight in enumerate((own, other)):
            pairs.append((weight.at[pl.ds(k * part, part)], weights.at[slot, which]))
        return [
            pltpu.make_async_copy(a, b, sems.at[slot, j]) for j, (a, b) in enumerate(pairs)
        ]

    for k in range(deep):
        for copy in copies(k):
            copy.start()
    for k in range(turns):
        for copy in copies(k):
            copy.wait()
        slot = k % deep
        wide = jnp.concatenate([block[slot, i] for i in range(chips)], axis=1)
        for which in range(CORES):
            more = jnp.dot(wide, weights[slot, which], preferred_element_type=f32)
            if k == 0:
                out[which] = more
            else:
                out[which] += more
        if k + deep < turns:
            for copy in copies(k + deep):
                copy.start()


def frozen_matmul(tokens, own, other):
    chips, count, both = tokens.shape
    width, wide = own.shape
    at_once = chips // TURNS
    shape = (CORES, count, wide)
    return pl.pallas_call(
        frozen_kernel,
        out_shape=jax.ShapeDtypeStruct(shape, f32),
        grid=(1,),
        in_specs=[pl.BlockSpec(memory_space=pl.ANY)] * 3,
        out_specs=pl.BlockSpec(shape, lambda k: (0, 0, 0)),
        scratch_shapes=[
            pltpu.VMEM((DEEP, at_once, count, both), bf16),
            pltpu.VMEM((DEEP, CORES, at_once * both, wide), bf16),
            pltpu.SemaphoreType.DMA((DEEP, 1 + CORES)),
        ],
        compiler_params=pltpu.CompilerParams(
            dimension_semantics=("arbitrary",), vmem_limit_bytes=56 << 20
        ),
        name="frozen",
    )(tokens, own, other)


def adapt_kernel(tile_seg, place, frozen, shrunk, own, other, own_out, other_out):
    parts, _, rank, _ = own.shape
    hidden = own_out.shape[1]
    tiles = own_out.shape[0] // TILE
    low = lax.broadcasted_iota(jnp.int32, (TILE, rank), 1) < rank // 2
    for t in range(tiles):
        seg = tile_seg[pl.program_id(0) * tiles + t]
        row = slice(t * TILE, (t + 1) * TILE)
        left = shrunk[:, row].astype(f32)
        gate_left = left[:rank].T.astype(bf16)
        up_left = left[rank:].T.astype(bf16)
        for which, (factors, out) in enumerate(((own, own_out), (other, other_out))):
            wide = jnp.concatenate([factors[m, seg] for m in range(parts)], axis=1)
            for_gate = jnp.dot(gate_left, wide, preferred_element_type=f32)
            for_up = jnp.dot(up_left, wide, preferred_element_type=f32)
            for a in range(parts // 2):
                even = slice(2 * a * rank, (2 * a + 1) * rank)
                odd = slice((2 * a + 1) * rank, (2 * a + 2) * rank)
                at = slice(a * rank, (a + 1) * rank)
                gate = jnp.where(
                    low, for_gate[:, even], pltpu.roll(for_gate[:, odd], rank // 2, 1)
                )
                up = jnp.where(low, pltpu.roll(for_up[:, even], rank // 2, 1), for_up[:, odd])
                gate = frozen[which, row, at] + adapter_scale * gate
                up = (
                    frozen[which, row, hidden + a * rank : hidden + (a + 1) * rank]
                    + adapter_scale * up
                )
                out[row, at] = (gate / (1.0 + jnp.exp(-gate)) * up).astype(bf16)


def adapt(frozen, shrunk, own, other, tile_seg, core):
    both, count, wide = frozen.shape
    rows = count // HALVES
    whole = pl.BlockSpec(own.shape, lambda i, seg, at: (0, 0, 0, 0))
    return pl.pallas_call(
        adapt_kernel,
        out_shape=[
            jax.ShapeDtypeStruct((CORES * count, wide // 2), bf16),
            jax.ShapeDtypeStruct((count, wide // 2), bf16),
        ],
        grid_spec=pltpu.PrefetchScalarGridSpec(
            num_scalar_prefetch=2,
            grid=(HALVES,),
            in_specs=[
                pl.BlockSpec((both, rows, wide), lambda i, seg, at: (0, i, 0)),
                pl.BlockSpec((shrunk.shape[0], rows), lambda i, seg, at: (0, i)),
                whole,
                whole,
            ],
            out_specs=[
                pl.BlockSpec((rows, wide // 2), lambda i, seg, at: (at[0] + i, 0)),
                pl.BlockSpec((rows, wide // 2), lambda i, seg, at: (i, 0)),
            ],
        ),
        compiler_params=pltpu.CompilerParams(
            dimension_semantics=("arbitrary",), vmem_limit_bytes=56 << 20
        ),
        name="adapt",
    )(tile_seg, (core * HALVES).reshape(1), frozen, shrunk, own, other)


def exchange(x, axes):
    return lax.all_to_all(x, axes, split_axis=0, concat_axis=0, tiled=True)


def swap(x):
    return lax.ppermute(x, "core", [(0, 1), (1, 0)])


def per_device(
    tokens,
    gate_up_weight,
    down_factor_pool,
    up_factor_pool,
    segment_adapters,
    segment_tile_counts,
    adapter_pool_rows,
):
    core = lax.axis_index("core")
    first = core == 0
    token_count, share = tokens.shape
    tile_count = token_count // TILE
    width = gate_up_weight.shape[0]
    wide = 2 * gate_up_weight.shape[2]
    twice_rank = down_factor_pool.shape[2]
    rank = twice_rank // 2
    segs = segment_adapters.shape[1]
    rows = token_count // CORES

    kept = lax.dynamic_slice_in_dim(tokens, core * rows, rows, axis=0)
    given = swap(lax.dynamic_slice_in_dim(tokens, (1 - core) * rows, rows, axis=0))
    start = jnp.where(
        first,
        jnp.concatenate([kept, given], axis=1),
        jnp.concatenate([given, kept], axis=1),
    )
    down_pool, start = lax.optimization_barrier((down_factor_pool[0], start))
    gathered = lax.all_gather(start, ("yhi", "ylo", "z"))
    gathered = gathered.reshape(SHARES // CORES, rows, CORES * share)

    cols = twice_rank // SHARES
    depth = rank + share // 2
    down_pool = down_pool.T.reshape(SHARES, cols, -1, share)
    down_pool = jnp.transpose(down_pool, (0, 2, 1, 3)).reshape(SHARES, depth - rank, share)
    pool = jnp.concatenate([up_factor_pool.reshape(SHARES, rank, rank), down_pool], axis=1)
    pool = exchange(pool, PLANE)

    w = gate_up_weight.reshape(YL * ZN * CORES, YH, share, wide)
    own_weight = jnp.transpose(w, (1, 0, 2, 3)).reshape(width, wide)
    pool, own_weight = lax.optimization_barrier((pool, own_weight))
    other_weight = swap(own_weight)

    chosen_rows = jnp.take(adapter_pool_rows, segment_adapters.reshape(-1), mode="clip")
    chosen = exchange(jnp.take(pool, chosen_rows, axis=0, mode="clip"), "grp")
    chosen = chosen.reshape(GRP, segs, depth, share)
    other_chosen = swap(chosen)
    columns = []
    for part in (jnp.where(first, chosen, other_chosen), jnp.where(first, other_chosen, chosen)):
        part = part[:, :, rank:].reshape(YL, GRP // YL, segs, -1, CORES, YH, cols, share)
        part = jnp.transpose(part, (2, 6, 5, 0, 1, 3, 4, 7)).reshape(segs, cols, width)
        columns.append(jnp.pad(part, ((0, 1), (0, SLOT - cols), (0, 0))).reshape(-1, width))
    columns = jnp.concatenate(columns)
    own_factors, other_factors = chosen[:, :, :rank], other_chosen[:, :, :rank]

    bounds = jnp.cumsum(segment_tile_counts[0])
    positions = jnp.arange(tile_count, dtype=jnp.int32)
    tile_seg = jnp.sum((bounds[None, :] <= positions[:, None]).astype(jnp.int32), axis=1)
    tile_seg = lax.dynamic_slice_in_dim(tile_seg, core * (tile_count // CORES), tile_count // CORES)

    columns, own_factors, other_factors, other_weight = lax.optimization_barrier(
        (columns, own_factors, other_factors, other_weight)
    )

    shrunk = exchange(shrink(gathered, columns, tile_seg, cols), CHIPS)
    shrunk = jnp.transpose(shrunk.reshape(YL * ZN, YH, CORES, cols, rows), (0, 2, 1, 3, 4))
    shrunk = shrunk.reshape(twice_rank, rows)

    frozen = frozen_matmul(gathered, own_weight, other_weight)
    hidden, for_other = adapt(frozen, shrunk, own_factors, other_factors, tile_seg, core)
    return lax.dynamic_update_slice_in_dim(hidden, swap(for_other), (1 - core) * rows, axis=0)


def solution(mesh):
    fine = Mesh(mesh.devices.reshape(GRP, YL, ZN, CORES, YH), AXES)
    return jax.shard_map(
        per_device,
        mesh=fine,
        in_specs=(
            P("grp", PLANE),
            P(None, None, PLANE),
            P(PLANE, "grp", None),
            P(PLANE, "grp", None, None, None),
            P(),
            P("grp", None),
            P(),
        ),
        out_specs=P("grp", PLANE),
        check_vma=False,
    )
```
